32 devices in a mesh: groups: 2 (over x), ctx: 16 (over z, y, core).
Axes of the slice: x: 2, y: 2, z: 4, core: 2. Of those that a mesh axis runs over, the one named last changes fastest.
Arguments:
- mixer_input: bfloat16 [2048, 8192], P(('groups', 'ctx')), parts along dimension 0, may hold values from -6 to 6
- gate_input: bfloat16 [2048, 8192], P(('groups', 'ctx')), parts along dimension 0, may hold values from -6 to 6
- step_raw: bfloat16 [2048, 8192], P(('groups', 'ctx')), parts along dimension 0, may hold values from -4 to 4
- input_proj: float32 [2048, 16], P(('groups', 'ctx')), parts along dimension 0, may hold values from -0.6 to 0.6
- output_proj: float32 [2048, 16], P(('groups', 'ctx')), parts along dimension 0, may hold values from -1.8 to 1.8
- decay_log: float32 [8192, 16], replicated, may hold values from -12 to 0
- conv_weight: float32 [8192, 4], replicated, may hold values from -3 to 3
- conv_bias: float32 [8192], replicated, may hold values from -3 to 3
- skip_gain: float32 [8192], replicated, may hold values from 0.5 to 1.5
- query_heads: bfloat16 [2048, 4096], P(('groups', 'ctx')), parts along dimension 0, may hold values from -6 to 6
- key_heads: bfloat16 [2048, 512], P(('groups', 'ctx')), parts along dimension 0, may hold values from -4 to 4
- value_heads: bfloat16 [2048, 512], P(('groups', 'ctx')), parts along dimension 0, may hold values from -6 to 6
Outputs:
- mixer_output: bfloat16 [2048, 8192], P(('groups', 'ctx')), parts along dimension 0
- attention: bfloat16 [2048, 4096], P(('groups', 'ctx')), parts along dimension 0
The draws below stay inside these ranges and needn't reach their ends.
There are 2 independent parts, one for each index of `groups`. The reference program is written for one: setup_inputs(seed, part) draws one part's arguments, and reference() takes and returns one part's arrays. A program takes and returns all parts, laid end to end along the dimension named above; an argument that names none is the same for every part. Nothing has to cross between parts.
All inputs are finite; a program needn't handle non-finite values.
Results may differ from the reference program's by a relative error of at most 0.0085.
Values may be sent and summed in bfloat16 or wider, within the bound.
A program may use at most 320 MiB of HBM per device.

```python
import math
import jax
import jax.numpy as jnp
from jax import lax

CH = 8192
STATE = 16
TAPS = 4
Q_HEADS = 32
KV_HEADS = 4
HEAD_DIM = 128
TOK_DEV = 64
SEQ = 1024


def draw_query_heads(key, part):
    shape_all = (SEQ, Q_HEADS * HEAD_DIM)
    probe_readings = jnp.clip(jax.random.normal(jax.random.fold_in(key, 1), shape_all, jnp.float32), -4.0, 4.0)
    return probe_readings.astype(jnp.bfloat16)


def draw_key_heads(key, part):
    shape_all = (SEQ, KV_HEADS * HEAD_DIM)
    probe_readings = jnp.clip(jax.random.normal(jax.random.fold_in(key, 2), shape_all, jnp.float32), -4.0, 4.0)
    return probe_readings.astype(jnp.bfloat16)


def draw_decay_log(key, part):
    slow_share = 0.5
    slow_level = jnp.exp(jax.random.uniform(jax.random.fold_in(key, 23), (CH,), jnp.float32, jnp.log(0.2), jnp.log(0.4)))
    slow_rate = slow_level / (TOK_DEV * 0.8)
    slow_pick = jax.random.bernoulli(jax.random.fold_in(key, 21), slow_share, (CH,))
    fast_rate = jnp.exp(jax.random.uniform(jax.random.fold_in(key, 22), (CH,), jnp.float32, jnp.log(0.025), jnp.log(0.05)))
    spread = jax.random.uniform(jax.random.fold_in(key, 24), (CH, STATE), jnp.float32, -0.7, 0.7)
    chosen = jnp.where(slow_pick, slow_rate, fast_rate)
    return (jnp.log(chosen)[:, None] + spread).astype(jnp.float32)


def draw_step_raw(key, part):
    shape_all = (SEQ, CH)
    noise = jnp.clip(0.5 * jax.random.normal(jax.random.fold_in(key, 31), shape_all, jnp.float32), -2.5, 2.5)
    position_offsets = jax.random.uniform(jax.random.fold_in(key, 32), (SEQ // TOK_DEV,), jnp.float32, -1.0, 1.0)
    element_indices = jnp.arange(SEQ)
    probe_readings = noise + position_offsets[element_indices // TOK_DEV][:, None]
    probe_indices = jax.random.randint(jax.random.fold_in(key, 33), (4,), 0, SEQ)
    packet_clusters = jnp.any(element_indices[:, None] == probe_indices[None, :], axis=1)
    probe_readings = jnp.where(packet_clusters[:, None], 4.0, probe_readings)
    return probe_readings.astype(jnp.bfloat16)


def levels(stream_key, extent, shards, least, top_value):
    def one(position, blocks):
        steps = jax.random.uniform(jax.random.fold_in(jax.random.fold_in(stream_key, 6), position), (blocks,), jnp.float32, least / len(shards), top_value / len(shards))
        return jnp.repeat(jnp.exp(steps), extent[position] // blocks).reshape((-1,) + (1,) * (len(extent) - position - 1))

    level = one(*shards[0])
    for cut in shards[1:]:
        level = level * one(*cut)
    return level


def centred(own_key, shape, width, limit, split=(), kind=jnp.bfloat16):
    level = levels(own_key, shape, split, -0.22, 0.18) if split else 1.0
    drawn = jax.random.normal(own_key, shape, jnp.float32) * width * level
    return jnp.minimum(jnp.maximum(drawn, -limit), limit).astype(kind)


def setup_inputs(seed: int = 0, part: int = 0) -> dict:
    seeds = jax.random.split(jax.random.key(seed), 13)
    own_keys = jax.random.split(jax.random.fold_in(seeds[12], part), 13)
    return {
        "mixer_input": centred(own_keys[0], (SEQ, CH), 1.0, 6.0, ((0, 16),)),
        "gate_input": centred(own_keys[1], (SEQ, CH), 1.0, 6.0, ((0, 16),)),
        "step_raw": draw_step_raw(jax.random.fold_in(jax.random.fold_in(seeds[12], part), 71), part),
        "input_proj": centred(own_keys[3], (SEQ, STATE), 0.1, 0.6, ((0, 16),), jnp.float32),
        "output_proj": centred(own_keys[4], (SEQ, STATE), 0.3, 1.8, ((0, 16),), jnp.float32),
        "decay_log": draw_decay_log(jax.random.fold_in(seeds[12], 71), part),
        "conv_weight": centred(seeds[6], (CH, TAPS), TAPS ** -0.5, 3.0, (), jnp.float32),
        "conv_bias": centred(seeds[7], (CH,), 0.5, 3.0, (), jnp.float32),
        "skip_gain": jnp.clip(jax.random.uniform(seeds[8], (CH,), jnp.float32, 0.5, 1.5), 0.5, 1.5),
        "query_heads": draw_query_heads(jax.random.fold_in(jax.random.fold_in(seeds[12], part), 71), part),
        "key_heads": draw_key_heads(jax.random.fold_in(jax.random.fold_in(seeds[12], part), 71), part),
        "value_heads": centred(own_keys[11], (SEQ, KV_HEADS * HEAD_DIM), 1.0, 6.0, ((0, 16),)),
    }


def reference(mixer_input, gate_input, step_raw, input_proj, output_proj, decay_log, conv_weight, conv_bias, skip_gain, query_heads, key_heads, value_heads):
    padded = jnp.concatenate([jnp.zeros((TAPS - 1, CH), jnp.bfloat16), mixer_input], axis=0)
    conv_sum = jnp.zeros((SEQ, CH), jnp.float32) + conv_bias[None, :]
    for tap_index in range(TAPS):
        conv_sum = conv_sum + conv_weight[:, tap_index][None, :] * padded[tap_index:tap_index + SEQ].astype(jnp.float32)
    inner_act = jax.nn.silu(conv_sum)
    step_size = jax.nn.softplus(step_raw.astype(jnp.float32))
    decay_rates = -jnp.exp(decay_log)

    def step_forward(hidden_state, items):
        step_now, inner_now, b_row, c_row = items
        decay_now = jnp.exp(step_now[:, None] * decay_rates)
        hidden_state = decay_now * hidden_state + (step_now * inner_now)[:, None] * b_row[None, :]
        return (hidden_state, lax.optimization_barrier(jnp.sum(hidden_state * c_row[None, :], axis=1)))
    final_state, scanned = lax.scan(step_forward, jnp.zeros((CH, STATE), jnp.float32), (step_size, inner_act, input_proj, output_proj))
    mixer_output = ((scanned + skip_gain[None, :] * inner_act) * jax.nn.silu(gate_input.astype(jnp.float32))).astype(jnp.bfloat16)
    groups_per = Q_HEADS // KV_HEADS
    block_rows = math.gcd(SEQ, 512)
    score_scale = 1.0 / math.sqrt(HEAD_DIM)
    queries4 = query_heads.reshape(SEQ, KV_HEADS, groups_per, HEAD_DIM)
    keys3 = key_heads.reshape(SEQ, KV_HEADS, HEAD_DIM)
    values3 = value_heads.reshape(SEQ, KV_HEADS, HEAD_DIM)
    key_places = jnp.arange(SEQ)

    def one_block(block_index):
        first_row = block_index * block_rows
        asker_panel_height = lax.dynamic_slice_in_dim(queries4, first_row, block_rows, 0)
        query_places = first_row + jnp.arange(block_rows)
        allowed = key_places[None, None, :] <= query_places[:, None, None]

        def one_head(head_index):
            query_head = asker_panel_height[:, head_index].astype(jnp.float32)
            key_head = keys3[:, head_index].astype(jnp.float32)
            value_head = values3[:, head_index].astype(jnp.float32)
            scores = jnp.einsum('tgd,sd->tgs', query_head, key_head) * score_scale
            scores = jnp.where(allowed, scores, -1e+30)
            largest = lax.optimization_barrier(jnp.max(scores, axis=2, keepdims=True))
            probs = jnp.where(allowed, jnp.exp(scores - largest), 0.0)
            totals = lax.optimization_barrier(jnp.sum(probs, axis=2))
            rounded = probs.astype(jnp.bfloat16).astype(jnp.float32)
            summed = jnp.einsum('tgs,sd->tgd', rounded, value_head)
            return summed / totals[:, :, None]
        per_head = lax.map(one_head, jnp.arange(KV_HEADS))
        return jnp.transpose(per_head, (1, 0, 2, 3))
    blocks = lax.map(one_block, jnp.arange(SEQ // block_rows))
    attention = blocks.reshape(SEQ, Q_HEADS * HEAD_DIM).astype(jnp.bfloat16)
    return (mixer_output, attention)
```

```python
import math

import jax
import jax.numpy as jnp
from jax import lax
from jax.experimental import pallas as pl
from jax.experimental.pallas import tpu as pltpu
from jax.sharding import PartitionSpec as P

STATE = 16
TAPS = 4
Q_HEADS = 32
KV_HEADS = 4
HEAD_DIM = 128
LANES = 128
SUB = 8
HALO = 16
BLOCK = 16
WIDE = 1024
PIECE = 512
CHUNK = 256
LINE = 4
KV_COLS = KV_HEADS * HEAD_DIM
PANEL = Q_HEADS // KV_HEADS * HEAD_DIM
LOG2E = math.log2(math.e)
MESH = pl.DeviceIdType.MESH
F32, BF16 = jnp.float32, jnp.bfloat16


def silu(v):
    return v / (1.0 + jnp.exp2(v * -LOG2E))


def split(v, pieces):
    out = []
    for _ in range(pieces):
        out.append(v.astype(BF16))
        v = v - out[-1].astype(F32)
    return out


def iota(shape, dim):
    return lax.broadcasted_iota(jnp.int32, shape, dim)


def spread(c_t, rows, state_major):
    depth = BLOCK * STATE
    n, k = iota((STATE, depth), 0), iota((STATE, depth), 1)
    pick = (k // BLOCK if state_major else k % STATE) == n
    tiled = lax.dot_general(
        c_t.astype(BF16), pick.astype(F32).astype(BF16), (((0,), (0,)), ((), ())), preferred_element_type=F32
    )
    t, k = iota((rows, depth), 0), iota((rows, depth), 1)
    own = (k % BLOCK if state_major else k // STATE) == t % BLOCK
    return jnp.where(own, tiled, 0.0).astype(BF16)


def mix_and_attend(
    x_hbm, raw_hbm, b_ref, c_ref, decay_hbm, w_ref, bias_ref, skip_ref, q_hbm, key_hbm, value_hbm,
    y_hbm, s_hbm, ent_hbm, out_hbm,
    xs, raws, rates, qs, kv, halo, step_s, u_s, y_s, sum_s, tot_s, b_s, c_s, hb0, hb1, hb2, hb3,
    snd, got, ans, lands, sbuf, att,
    in_x, in_raw, in_misc, own_kv, halo_send, halo_recv,
    kv_recv, kv_up, kv_dn, kv_y, kv_core, send_a, recv_a, send_b, recv_b, out_y, out_s, out_a, out_e,
):
    rows, channels = x_hbm.shape
    size, _, message = got.shape
    owners = snd.shape[0]
    share = message - LANES
    groups = channels // WIDE
    per_group = WIDE // share
    line = size // LINE
    tiles = WIDE // LANES
    me = lax.axis_index("ctx")
    z, within = me // LINE, me % LINE
    y, core = within // 2, within % 2
    across = me + 2 - 4 * y
    sibling = me + 1 - 2 * core
    barrier = pltpu.get_barrier_semaphore()

    def greet(off, _):
        pl.semaphore_signal(
            barrier, inc=1, device_id={"ctx": lax.rem(me + off, size)}, device_id_type=MESH
        )
        return 0

    lax.fori_loop(1, size, greet, 0)

    def wide(g):
        return pl.ds(pl.multiple_of(g * WIDE, WIDE), WIDE)

    def load_x(g):
        return pltpu.make_async_copy(x_hbm.at[:, wide(g)], xs.at[:, wide(g)], in_x.at[g])

    def load_raw(g):
        return pltpu.make_async_copy(raw_hbm.at[:, wide(g)], raws.at[:, wide(g)], in_raw.at[g])

    def slot(d):
        return pl.ds(pl.multiple_of(d * rows, rows), rows)

    own_copies = [
        pltpu.make_async_copy(
            source, kv.at[slot(me), pl.ds(i * KV_COLS, KV_COLS)], own_kv.at[i]
        )
        for i, source in enumerate((key_hbm, value_hbm))
    ]
    misc = [
        pltpu.make_async_copy(decay_hbm, rates, in_misc.at[0]),
        pltpu.make_async_copy(q_hbm, qs, in_misc.at[1]),
    ]

    def start_loads(g, _):
        load_raw(g).start()
        load_x(g).start()
        return 0

    lax.fori_loop(0, groups, start_loads, 0)
    for copy in own_copies + misc:
        copy.start()

    def halo_copy(to):
        return pltpu.make_async_remote_copy(
            src_ref=x_hbm.at[pl.ds(rows - HALO, HALO), :],
            dst_ref=halo,
            send_sem=halo_send,
            recv_sem=halo_recv,
            device_id={"ctx": to},
            device_id_type=MESH,
        )

    def kv_copy(origin, to, send_sem):
        return pltpu.make_async_remote_copy(
            src_ref=kv.at[slot(origin), :],
            dst_ref=kv.at[slot(origin), :],
            send_sem=send_sem,
            recv_sem=kv_recv.at[origin],
            device_id={"ctx": to},
            device_id_type=MESH,
        )

    def go_up(origin):
        return kv_copy(origin, me + LINE, kv_up.at[origin // LINE])

    def go_down(origin):
        return kv_copy(origin, me - LINE, kv_dn.at[origin // LINE])

    def go_across(origin):
        return kv_copy(origin, across, kv_y.at[origin // LINE])

    def go_core(origin):
        return kv_copy(origin, sibling, kv_core.at[origin // 2])

    def arrived(origin):
        kv_copy(origin, sibling, kv_core.at[origin // 2]).wait_recv()

    def relay(j):
        below, above = me - LINE * j, me + LINE * j

        @pl.when(below >= 0)
        def _():
            arrived(below)

            @pl.when(z < line - 1)
            def _():
                go_up(below).start()

            go_across(below).start()
            go_core(below).start()

        @pl.when(above < size)
        def _():
            arrived(above)

            @pl.when(z > 0)
            def _():
                go_down(above).start()

            go_across(above).start()
            go_core(above).start()

    def cross(j):
        below, above = across - LINE * j, across + LINE * j

        @pl.when(below >= 0)
        def _():
            arrived(below)
            go_core(below).start()

        @pl.when(jnp.logical_and(above < size, j > 0))
        def _():
            arrived(above)
            go_core(above).start()

    def kv_step(j, _):
        relay(j)
        cross(j - 1)
        return 0

    b_t = b_ref[...]
    for t in range(rows):
        b_s[pl.ds(t * STATE, STATE), :] = jnp.broadcast_to(b_t[:, t : t + 1], (STATE, LANES))
    c_s[...] = spread(c_ref[...], rows, False)

    pl.semaphore_wait(barrier, size - 1)

    @pl.when(me + 1 < size)
    def _():
        halo_copy(me + 1).start()

    for copy in own_copies:
        copy.wait()

    @pl.when(z < line - 1)
    def _():
        go_up(me).start()

    @pl.when(z > 0)
    def _():
        go_down(me).start()

    go_across(me).start()
    go_core(me).start()

    lower = (iota((rows, rows), 0) >= iota((rows, rows), 1)).astype(F32).astype(BF16)

    def shifts(height, depth, first):
        r, c = iota(((TAPS - 1) * height, depth), 0), iota(((TAPS - 1) * height, depth), 1)
        return (c == first + r % height - r // height - 1).astype(F32).astype(BF16)

    def convolve(cols, source, shift, height, first):
        moved = jnp.dot(shift, source, preferred_element_type=F32)
        conv = bias_ref[:, cols] + w_ref[pl.ds(TAPS - 1, 1), cols] * source[first : first + height].astype(F32)
        for back in range(1, TAPS):
            conv = conv + w_ref[pl.ds(TAPS - 1 - back, 1), cols] * moved[(back - 1) * height : back * height]
        return silu(conv)

    per_wide = WIDE // PIECE
    full_shift = shifts(rows, rows, 0)

    def prepare(i, _):
        g = i // per_wide

        @pl.when(i % per_wide == 0)
        def _():
            load_x(g).wait()
            load_raw(g).wait()

        cols = pl.ds(pl.multiple_of(i * PIECE, PIECE), PIECE)
        inside = pl.ds(pl.multiple_of((i % per_wide) * PIECE, PIECE), PIECE)
        step = jnp.log(1.0 + jnp.exp2(raws[:, cols].astype(F32) * LOG2E))
        high, low = split(step, 2)
        sums = jnp.dot(lower, high, preferred_element_type=F32) + jnp.dot(
            lower, low, preferred_element_type=F32
        )
        step_s[:, cols] = step
        sum_s[g, :, inside] = sums.astype(BF16)
        tot_s[:, cols] = sums[rows - 1 :]
        inner = convolve(cols, xs[:, cols], full_shift, rows, 0)
        u_s[:, cols] = step * inner
        y_s[g, :, inside] = skip_ref[:, cols] * inner
        return 0

    lax.fori_loop(0, channels // PIECE, prepare, 0)

    misc[0].wait()

    def scale_rates(i, _):
        cols = pl.ds(pl.multiple_of(i * WIDE, WIDE), WIDE)
        rates[:, cols] = -LOG2E * jnp.exp2(rates[:, cols] * LOG2E)
        return 0

    lax.fori_loop(0, groups, scale_rates, 0)

    @pl.when(me > 0)
    def _():
        halo_copy(me).wait_recv()
        edge_shift = shifts(SUB, 2 * HALO, HALO)

        def edge(i, _):
            g = i // per_wide
            cols = pl.ds(pl.multiple_of(i * PIECE, PIECE), PIECE)
            inside = pl.ds(pl.multiple_of((i % per_wide) * PIECE, PIECE), PIECE)
            source = jnp.concatenate([halo[:, cols], xs[pl.ds(0, HALO), cols]], axis=0)
            inner = convolve(cols, source, edge_shift, SUB, HALO)
            top = pl.ds(0, SUB)
            u_s[top, cols] = step_s[top, cols] * inner
            y_s[g, top, inside] = skip_ref[:, cols] * inner
            return 0

        lax.fori_loop(0, channels // PIECE, edge, 0)

    def ask(to, origin):
        return pltpu.make_async_remote_copy(
            src_ref=snd.at[to],
            dst_ref=got.at[origin],
            send_sem=send_a.at[to],
            recv_sem=recv_a.at[origin],
            device_id={"ctx": to},
            device_id_type=MESH,
        )

    def answer(to, origin):
        return pltpu.make_async_remote_copy(
            src_ref=ans.at[to],
            dst_ref=lands.at[origin],
            send_sem=send_b.at[to],
            recv_sem=recv_b.at[origin],
            device_id={"ctx": to},
            device_id_type=MESH,
        )

    def put_y(g):
        return pltpu.make_async_copy(y_s.at[g], y_hbm.at[g], out_y.at[g])

    def put_s(g):
        return pltpu.make_async_copy(sum_s.at[g], s_hbm.at[g], out_s.at[g])

    buffers = (hb0, hb1, hb2, hb3)
    zero = jnp.zeros((SUB, LANES), F32)

    def scan_group(g, _):
        left = g * WIDE
        cols = [pl.ds(pl.multiple_of(left + k * LANES, LANES), LANES) for k in range(tiles)]
        lax.fori_loop(done_steps(g - 1) + 1, done_steps(g) + 1, kv_step, 0)
        put_s(g).start()
        hs = [zero] * (2 * tiles)
        for block in range(rows // BLOCK):
            first = block * BLOCK
            buffer = buffers[block % len(buffers)]
            for i in range(BLOCK):
                t = first + i
                b = [b_s[pl.ds(t * STATE + half * SUB, SUB), :] for half in range(2)]
                for k in range(tiles):
                    step = jnp.broadcast_to(step_s[pl.ds(t, 1), cols[k]], (SUB, LANES))
                    u = jnp.broadcast_to(u_s[pl.ds(t, 1), cols[k]], (SUB, LANES))
                    for half in range(2):
                        at = 2 * k + half
                        decay = jnp.exp2(step * rates[pl.ds(half * SUB, SUB), cols[k]])
                        hs[at] = decay * hs[at] + u * b[half]
                    buffer[k, pl.ds(i * STATE, STATE), :] = jnp.concatenate(
                        [hs[2 * k], hs[2 * k + 1]], axis=0
                    ).astype(BF16)
            for k in range(0, tiles, 2):
                pair = jnp.concatenate([buffer[k], buffer[k + 1]], axis=1)
                at = (g, pl.ds(first, BLOCK), pl.ds(k * LANES, 2 * LANES))
                y_s[at] = y_s[at] + jnp.dot(
                    c_s[pl.ds(first, BLOCK), :], pair, preferred_element_type=F32
                )
        put_y(g).start()
        across_share = share // LANES
        filler = jnp.zeros((STATE - 3 * across_share, LANES), F32)
        for part in range(per_group):
            to = g * per_group + part
            pieces = [[], [], []]
            for k in range(across_share):
                tile = part * across_share + k
                snd[to, :, pl.ds(k * LANES, LANES)] = jnp.concatenate(
                    [hs[2 * tile], hs[2 * tile + 1]], axis=0
                ).astype(BF16)
                for p, piece in enumerate(split(tot_s[:, cols[tile]], 3)):
                    pieces[p].append(piece.astype(F32))
            snd[to, :, pl.ds(share, LANES)] = jnp.concatenate(
                pieces[0] + pieces[1] + pieces[2] + [filler], axis=0
            ).astype(BF16)

            @pl.when(to != me)
            def _():
                ask(to, me).start()

        return 0

    def done_steps(g):
        return jnp.where(g < 0, 0, jnp.minimum(line - 1, ((line - 1) * (g + 2)) // (groups - 1)))

    lax.fori_loop(0, groups, scan_group, 0)
    cross(line - 1)

    misc[1].wait()

    def all_arrived(i, _):
        arrived(2 * i + 1 - core)
        return 0

    lax.fori_loop(0, size // 2, all_arrived, 0)

    heads = PANEL // HEAD_DIM
    scale = LOG2E / math.sqrt(HEAD_DIM)
    wide_q = heads * rows
    full = (me * rows) // CHUNK

    def put_att(h):
        at = pl.ds(pl.multiple_of(h * PANEL, PANEL), PANEL)
        return pltpu.make_async_copy(att.at[:, at], out_hbm.at[:, at], out_a.at[h])

    def attend(h, _):
        q = jnp.concatenate(
            [
                qs[:, pl.ds(pl.multiple_of(h * PANEL + j * HEAD_DIM, HEAD_DIM), HEAD_DIM)]
                for j in range(heads)
            ],
            axis=0,
        )
        k_cols = pl.ds(pl.multiple_of(h * HEAD_DIM, HEAD_DIM), HEAD_DIM)
        v_cols = pl.ds(pl.multiple_of(KV_COLS + h * HEAD_DIM, HEAD_DIM), HEAD_DIM)

        def score(c, top, masked):
            at = pl.ds(pl.multiple_of(c * CHUNK, CHUNK), CHUNK)
            s = lax.dot_general(
                kv[at, k_cols], q, (((1,), (1,)), ((), ())), preferred_element_type=F32
            )
            if masked:
                place = c * CHUNK + iota((CHUNK, wide_q), 0)
                asker = me * rows + iota((CHUNK, wide_q), 1) % rows
                s = jnp.where(place <= asker, s, -1e30)
            sbuf[at, :] = s
            return jnp.maximum(top, jnp.max(s.reshape(CHUNK // SUB, SUB, wide_q), axis=0))

        top = jnp.full((SUB, wide_q), -1e30, F32)
        top = lax.fori_loop(0, full, lambda c, m: score(c, m, False), top)
        top = score(full, top, True)
        top = jnp.max(top, axis=0, keepdims=True) * scale

        def weigh(c, carry):
            total, summed = carry
            at = pl.ds(pl.multiple_of(c * CHUNK, CHUNK), CHUNK)
            probs = jnp.exp2(sbuf[at, :] * scale - top)
            total = total + jnp.sum(probs.reshape(CHUNK // SUB, SUB, wide_q), axis=0)
            summed = summed + lax.dot_general(
                kv[at, v_cols], probs.astype(BF16), (((0,), (0,)), ((), ())), preferred_element_type=F32
            )
            return total, summed

        total, summed = lax.fori_loop(
            0, full + 1, weigh, (jnp.zeros((SUB, wide_q), F32), jnp.zeros((HEAD_DIM, wide_q), F32))
        )
        out = (summed / jnp.sum(total, axis=0, keepdims=True)).T.astype(BF16)
        for j in range(heads):
            att[:, pl.ds(pl.multiple_of(h * PANEL + j * HEAD_DIM, HEAD_DIM), HEAD_DIM)] = out[
                j * rows : (j + 1) * rows
            ]
        put_att(h).start()
        return 0

    early = 1
    lax.fori_loop(0, early, attend, 0)

    def join(d, hs):
        @pl.when(d != me)
        def _():
            ask(d, d).wait_recv()

        across_share = share // LANES
        parts = got[d, :, pl.ds(share, LANES)].astype(F32)
        new = []
        for k in range(across_share):
            lane = pl.ds(k * LANES, LANES)
            ans[d, :, lane] = hs[k].astype(BF16)
            total = (
                parts[k : k + 1] + parts[across_share + k : across_share + k + 1]
            ) + parts[2 * across_share + k : 2 * across_share + k + 1]
            rate = rates[:, pl.ds(pl.multiple_of(me * share + k * LANES, LANES), LANES)]
            new.append(jnp.exp2(rate * total) * hs[k] + got[d, :, lane].astype(F32))

        @pl.when(d != me)
        def _():
            answer(d, me).start()

        return tuple(new)

    @pl.when(me < owners)
    def _():
        got[me] = snd[me]
        lax.fori_loop(0, size, join, (jnp.zeros((STATE, LANES), F32),) * (share // LANES))
        lands[me] = ans[me]

    lax.fori_loop(early, KV_HEADS, attend, 0)

    def asked(to, _):
        @pl.when(to != me)
        def _():
            ask(to, to).wait_send()
            answer(to, to).wait_recv()

        return 0

    lax.fori_loop(0, owners, asked, 0)
    entering = pltpu.make_async_copy(lands, ent_hbm, out_e)
    entering.start()

    @pl.when(me < owners)
    def _():
        def answered(to, _):
            @pl.when(to != me)
            def _():
                answer(to, to).wait_send()

            return 0

        lax.fori_loop(0, size, answered, 0)

    @pl.when(me + 1 < size)
    def _():
        halo_copy(me + 1).wait_send()

    def sent(i, _):
        mine = i * LINE + within

        @pl.when(jnp.logical_and(i <= z, z < line - 1))
        def _():
            go_up(mine).wait_send()

        @pl.when(jnp.logical_and(i >= z, z > 0))
        def _():
            go_down(mine).wait_send()

        go_across(mine).wait_send()
        go_core(mine).wait_send()
        go_core(i * LINE + 2 - 2 * y + core).wait_send()
        return 0

    lax.fori_loop(0, line, sent, 0)

    def written(g, _):
        put_y(g).wait()
        put_s(g).wait()
        return 0

    lax.fori_loop(0, groups, written, 0)

    def att_written(h, _):
        put_att(h).wait()
        return 0

    lax.fori_loop(0, KV_HEADS, att_written, 0)
    entering.wait()


def correct(y_ref, s_ref, ent_ref, decay_ref, c_ref, gate_ref, out_ref, rate_s, ent_s, c_s):
    rows = gate_ref.shape[0]
    parts, _, share = ent_ref.shape
    group = pl.program_id(0)

    @pl.when(group == 0)
    def _():
        c_s[...] = spread(c_ref[...], rows, True)

    rate_s[...] = -LOG2E * jnp.exp2(decay_ref[...] * LOG2E)
    for part in range(parts):
        ent_s[:, pl.ds(part * share, share)] = ent_ref[part].astype(F32)

    def one(i, _):
        sides = [
            pl.ds(pl.multiple_of(i * 2 * LANES + side * LANES, LANES), LANES) for side in range(2)
        ]
        both = pl.ds(pl.multiple_of(i * 2 * LANES, 2 * LANES), 2 * LANES)
        blocks = rows // BLOCK
        grown = [[[] for _ in range(2)] for _ in range(blocks)]
        for side in range(2):
            sums = [s_ref[0, pl.ds(block * BLOCK, BLOCK), sides[side]] for block in range(blocks)]
            for n in range(STATE):
                rate = jnp.broadcast_to(rate_s[pl.ds(n, 1), sides[side]], (BLOCK, LANES)).astype(BF16)
                ent = jnp.broadcast_to(ent_s[pl.ds(n, 1), sides[side]], (BLOCK, LANES)).astype(BF16)
                for block in range(blocks):
                    grown[block][side].append(jnp.exp2(sums[block] * rate) * ent)
        for block in range(blocks):
            at = pl.ds(block * BLOCK, BLOCK)
            right = jnp.concatenate(
                [jnp.concatenate(grown[block][side], axis=0) for side in range(2)], axis=1
            )
            total = y_ref[0, at, both] + jnp.dot(c_s[at, :], right, preferred_element_type=F32)
            out_ref[at, both] = (total * silu(gate_ref[at, both].astype(F32))).astype(BF16)
        return 0

    lax.fori_loop(0, WIDE // (2 * LANES), one, 0)


def per_device(
    mixer_input,
    gate_input,
    step_raw,
    input_proj,
    output_proj,
    decay_log,
    conv_weight,
    conv_bias,
    skip_gain,
    query_heads,
    key_heads,
    value_heads,
):
    rows, channels = mixer_input.shape
    size = lax.axis_size("ctx")
    groups = channels // WIDE
    line = size // LINE
    share = max(LANES, channels // size)
    owners = channels // share
    keys = rows * size
    shape = jax.ShapeDtypeStruct
    anywhere = pl.BlockSpec(memory_space=pl.ANY)
    whole = pl.BlockSpec(memory_space=pltpu.VMEM)
    dma = pltpu.SemaphoreType.DMA
    hbuf = pltpu.VMEM((WIDE // LANES, BLOCK * STATE, LANES), BF16)
    decay = decay_log.T
    c_t = output_proj.T

    y, sums, entering, attention = pl.pallas_call(
        mix_and_attend,
        in_specs=[anywhere, anywhere, whole, whole, anywhere, whole, whole, whole]
        + [anywhere] * 3,
        out_specs=[anywhere] * 4,
        out_shape=[
            shape((groups, rows, WIDE), F32),
            shape((groups, rows, WIDE), BF16),
            shape((owners, STATE, share), BF16),
            shape((rows, Q_HEADS * HEAD_DIM), BF16),
        ],
        scratch_shapes=[
            pltpu.VMEM((rows, channels), BF16),
            pltpu.VMEM((rows, channels), BF16),
            pltpu.VMEM((STATE, channels), F32),
            pltpu.VMEM((rows, Q_HEADS * HEAD_DIM), BF16),
            pltpu.VMEM((keys, 2 * KV_COLS), BF16),
            pltpu.VMEM((HALO, channels), BF16),
            pltpu.VMEM((rows, channels), F32),
            pltpu.VMEM((rows, channels), F32),
            pltpu.VMEM((groups, rows, WIDE), F32),
            pltpu.VMEM((groups, rows, WIDE), BF16),
            pltpu.VMEM((1, channels), F32),
            pltpu.VMEM((rows * STATE, LANES), F32),
            pltpu.VMEM((rows, BLOCK * STATE), BF16),
            hbuf,
            hbuf,
            hbuf,
            hbuf,
            pltpu.VMEM((owners, STATE, share + LANES), BF16),
            pltpu.VMEM((size, STATE, share + LANES), BF16),
            pltpu.VMEM((size, STATE, share), BF16),
            pltpu.VMEM((owners, STATE, share), BF16),
            pltpu.VMEM((keys, PANEL // HEAD_DIM * rows), F32),
            pltpu.VMEM((rows, Q_HEADS * HEAD_DIM), BF16),
            dma((groups,)),
            dma((groups,)),
            dma((2,)),
            dma((2,)),
            dma,
            dma,
            dma((size,)),
            dma((line,)),
            dma((line,)),
            dma((line,)),
            dma((2 * line,)),
            dma((owners,)),
            dma((size,)),
            dma((size,)),
            dma((owners,)),
            dma((groups,)),
            dma((groups,)),
            dma((KV_HEADS,)),
            dma,
        ],
        compiler_params=pltpu.CompilerParams(
            collective_id=0, has_side_effects=True, vmem_limit_bytes=60 * 2**20
        ),
        cost_estimate=pl.CostEstimate(
            flops=8 * rows * channels * STATE,
            bytes_accessed=8 * rows * channels,
            transcendentals=rows * channels * STATE,
        ),
        name="mix_and_attend",
    )(
        mixer_input, step_raw, input_proj.T, c_t, decay, conv_weight.T, conv_bias[None], skip_gain[None],
        query_heads, key_heads, value_heads,
    )

    parts = WIDE // share
    wide = pl.BlockSpec((rows, WIDE), lambda g: (0, g))
    slab = pl.BlockSpec((1, rows, WIDE), lambda g: (g, 0, 0))
    mixer_output = pl.pallas_call(
        correct,
        grid=(groups,),
        in_specs=[
            slab,
            slab,
            pl.BlockSpec((parts, STATE, share), lambda g: (g, 0, 0)),
            pl.BlockSpec((STATE, WIDE), lambda g: (0, g)),
            pl.BlockSpec((STATE, rows), lambda g: (0, 0)),
            wide,
        ],
        out_specs=wide,
        out_shape=shape((rows, channels), BF16),
        scratch_shapes=[
            pltpu.VMEM((STATE, WIDE), F32),
            pltpu.VMEM((STATE, WIDE), F32),
            pltpu.VMEM((rows, BLOCK * STATE), BF16),
        ],
        cost_estimate=pl.CostEstimate(
            flops=4 * rows * channels * STATE,
            bytes_accessed=12 * rows * channels,
            transcendentals=rows * channels * STATE,
        ),
        name="correct",
    )(y, sums, entering, decay, c_t, gate_input)
    return (mixer_output, attention)


def solution(mesh):
    tokens = P(("groups", "ctx"), None)
    in_specs = (tokens,) * 5 + (P(),) * 4 + (tokens,) * 3
    return jax.shard_map(
        per_device, mesh=mesh, in_specs=in_specs, out_specs=(tokens, tokens), check_vma=False
    )
```

```python
import math

import jax
import jax.numpy as jnp
from jax import lax
from jax.experimental import pallas as pl
from jax.experimental.pallas import tpu as pltpu
from jax.sharding import PartitionSpec as P

STATE = 16
TAPS = 4
Q_HEADS = 32
KV_HEADS = 4
HEAD_DIM = 128
LANES = 128
SUB = 8
HALO = 16
BLOCK = 16
WIDE = 1024
EARLY = 3
CHUNK = 256
LINE = 4
KV_COLS = KV_HEADS * HEAD_DIM
PANEL = Q_HEADS // KV_HEADS * HEAD_DIM
LOG2E = math.log2(math.e)
MESH = pl.DeviceIdType.MESH
F32, BF16 = jnp.float32, jnp.bfloat16


def silu(v):
    return v / (1.0 + jnp.exp2(v * -LOG2E))


def split(v, pieces):
    out = []
    for _ in range(pieces):
        out.append(v.astype(BF16))
        v = v - out[-1].astype(F32)
    return out


def iota(shape, dim):
    return lax.broadcasted_iota(jnp.int32, shape, dim)


def spread(c_t, rows):
    depth = BLOCK * STATE
    pick = iota((STATE, depth), 1) % STATE == iota((STATE, depth), 0)
    tiled = lax.dot_general(
        c_t.astype(BF16), pick.astype(F32).astype(BF16), (((0,), (0,)), ((), ())), preferred_element_type=F32
    )
    own = iota((rows, depth), 1) // STATE == iota((rows, depth), 0) % BLOCK
    return jnp.where(own, tiled, 0.0).astype(BF16)


def mix_and_attend(
    x_hbm, raw_hbm, gate_hbm, b_ref, c_ref, decay_hbm, w_ref, bias_ref, skip_ref, q_hbm, key_hbm, value_hbm,
    mixed_hbm, out_hbm,
    xs, raws, rates, qs, kv, rim, halo, step_s, u_s, y_s, sum_s, b_s, c_s, decays, hb0, hb1, hb2, hb3,
    snd, got, ans, lands, sbuf, att,
    in_x, in_raw, in_gate, in_misc, own_kv, halo_send, halo_recv,
    kv_recv, kv_up, kv_dn, kv_y, kv_core, send_a, recv_a, send_b, recv_b, out_y, out_a,
):
    rows, channels = x_hbm.shape
    halves, size, part, _, _ = ans.shape
    kept = decays.shape[0] > 1
    owners = lands.shape[1]
    groups = channels // WIDE
    line = size // LINE
    tiles = WIDE // LANES
    lap = owners // tiles
    me = lax.axis_index("ctx")
    z, within = me // LINE, me % LINE
    y, core = within // 2, within % 2
    across = me + 2 - 4 * y
    sibling = me + 1 - 2 * core
    barrier = pltpu.get_barrier_semaphore()

    def greet(off, _):
        pl.semaphore_signal(
            barrier, inc=1, device_id={"ctx": lax.rem(me + off, size)}, device_id_type=MESH
        )
        return 0

    lax.fori_loop(1, size, greet, 0)

    def wide(g):
        return pl.ds(pl.multiple_of(g * WIDE, WIDE), WIDE)

    def load_x(g):
        return pltpu.make_async_copy(x_hbm.at[:, wide(g)], xs.at[:, wide(g)], in_x.at[g])

    def load_raw(g):
        return pltpu.make_async_copy(raw_hbm.at[:, wide(g)], raws.at[:, wide(g)], in_raw.at[g])

    def load_gate(g):
        return pltpu.make_async_copy(gate_hbm.at[:, wide(g)], raws.at[:, wide(g)], in_gate.at[g])

    def slot(d):
        return pl.ds(pl.multiple_of(d * rows, rows), rows)

    own_copies = [
        pltpu.make_async_copy(
            source, kv.at[slot(me), pl.ds(i * KV_COLS, KV_COLS)], own_kv.at[i]
        )
        for i, source in enumerate((key_hbm, value_hbm))
    ]
    misc = [
        pltpu.make_async_copy(decay_hbm, rates, in_misc.at[0]),
        pltpu.make_async_copy(q_hbm, qs, in_misc.at[1]),
    ]

    def start_loads(g, _):
        load_raw(g).start()
        load_x(g).start()
        return 0

    lax.fori_loop(0, groups, start_loads, 0)
    for copy in own_copies + misc:
        copy.start()

    def halo_copy(to):
        return pltpu.make_async_remote_copy(
            src_ref=rim,
            dst_ref=halo,
            send_sem=halo_send,
            recv_sem=halo_recv,
            device_id={"ctx": to},
            device_id_type=MESH,
        )

    def kv_copy(origin, to, send_sem):
        return pltpu.make_async_remote_copy(
            src_ref=kv.at[slot(origin), :],
            dst_ref=kv.at[slot(origin), :],
            send_sem=send_sem,
            recv_sem=kv_recv.at[origin],
            device_id={"ctx": to},
            device_id_type=MESH,
        )

    def go_up(j):
        return kv_copy(me, me + LINE * j, kv_up.at[j])

    def go_down(j):
        return kv_copy(me, me - LINE * j, kv_dn.at[j])

    def go_across(origin):
        return kv_copy(origin, across, kv_y.at[origin // LINE])

    def go_core(origin):
        return kv_copy(origin, sibling, kv_core.at[origin // 2])

    def arrived(origin):
        kv_copy(origin, sibling, kv_core.at[origin // 2]).wait_recv()

    def along(j, act):
        @pl.when(z + j < line)
        def _():
            act(go_up(j))

        @pl.when(z - j >= 0)
        def _():
            act(go_down(j))

    def relay(origin):
        arrived(origin)
        go_across(origin).start()
        go_core(origin).start()

    def cross(origin):
        arrived(origin)
        go_core(origin).start()

    def kv_step(j, _):
        below, above = me - LINE * j, me + LINE * j
        pl.when(jnp.logical_and(j < line, below >= 0))(lambda: relay(below))
        pl.when(jnp.logical_and(j < line, above < size))(lambda: relay(above))
        below, above = across - LINE * (j - 2), across + LINE * (j - 2)
        pl.when(jnp.logical_and(j >= 2, below >= 0))(lambda: cross(below))
        pl.when(jnp.logical_and(j > 2, above < size))(lambda: cross(above))
        return 0

    def done_steps(g):
        return ((line + 1) * (g + 2)) // (groups + 2)

    b_t = b_ref[...]
    for t in range(rows):
        b_s[pl.ds(t * STATE, STATE), :] = jnp.broadcast_to(b_t[:, t : t + 1], (STATE, LANES))
    c_s[...] = spread(c_ref[...], rows)

    def x_ready(g, _):
        load_x(g).wait()
        return 0

    lax.fori_loop(0, groups, x_ready, 0)
    last = xs[pl.ds(rows - HALO, HALO), :].astype(F32)
    rim_rows = [
        last[HALO - TAPS + 1 + r : HALO - TAPS + 2 + r, g * WIDE : (g + 1) * WIDE]
        for r in range(TAPS - 1)
        for g in range(groups)
    ]
    rim_rows.append(jnp.zeros((rim.shape[0] - len(rim_rows), WIDE), F32))
    rim[...] = jnp.concatenate(rim_rows, axis=0).astype(BF16)

    pl.semaphore_wait(barrier, size - 1)

    @pl.when(me + 1 < size)
    def _():
        halo_copy(me + 1).start()

    for copy in own_copies:
        copy.wait()

    go_across(me).start()
    go_core(me).start()

    def send_along(j, _):
        along(j, lambda copy: copy.start())
        return 0

    lax.fori_loop(1, line, send_along, 0)

    def shifts(height, depth, first):
        r, c = iota(((TAPS - 1) * height, depth), 0), iota(((TAPS - 1) * height, depth), 1)
        return (c == first + r % height - r // height - 1).astype(F32).astype(BF16)

    def convolve(cols, source, shift, height, first):
        moved = jnp.dot(shift, source, preferred_element_type=F32)
        conv = bias_ref[:, cols] + w_ref[pl.ds(TAPS - 1, 1), cols] * source[first : first + height].astype(F32)
        for back in range(1, TAPS):
            conv = conv + w_ref[pl.ds(TAPS - 1 - back, 1), cols] * moved[(back - 1) * height : back * height]
        return silu(conv)

    full_shift = shifts(rows, rows, 0)

    def prepare(g, _):
        load_raw(g).wait()
        cols = wide(g)
        step = jnp.log(1.0 + jnp.exp2(raws[:, cols].astype(F32) * LOG2E))
        step_s[:, cols] = step
        left = jnp.sum(step, axis=0, keepdims=True)
        for p in range(3):
            piece = left.astype(BF16).astype(F32)
            sum_s[pl.ds(p, 1), cols] = piece
            left = left - piece
        inner = convolve(cols, xs[:, cols], full_shift, rows, 0)
        u_s[:, cols] = step * inner
        y_s[g] = skip_ref[:, cols] * inner
        load_gate(g).start()
        return 0

    lax.fori_loop(0, groups, prepare, 0)
    misc[0].wait()

    def scale_rates(i, _):
        cols = pl.ds(pl.multiple_of(i * WIDE, WIDE), WIDE)
        rates[:, cols] = -LOG2E * jnp.exp2(rates[:, cols] * LOG2E)
        return 0

    lax.fori_loop(0, groups, scale_rates, 0)

    @pl.when(me > 0)
    def _():
        halo_copy(me).wait_recv()
        edge_shift = shifts(SUB, 2 * HALO, HALO)
        before = halo[...].astype(F32)
        for g in range(groups):
            cols = pl.ds(g * WIDE, WIDE)
            source = jnp.concatenate(
                [jnp.zeros((HALO - TAPS + 1, WIDE), F32)]
                + [before[r * groups + g : r * groups + g + 1] for r in range(TAPS - 1)],
                axis=0,
            ).astype(BF16)
            source = jnp.concatenate([source, xs[pl.ds(0, HALO), cols]], axis=0)
            inner = convolve(cols, source, edge_shift, SUB, HALO)
            top = pl.ds(0, SUB)
            u_s[top, cols] = step_s[top, cols] * inner
            y_s[g, top, :] = skip_ref[:, cols] * inner

    def home(owner):
        return (owner % tiles) * lap + owner // tiles

    owner_me = (me % lap) * tiles + me // lap

    def ask(half, owner, origin):
        return pltpu.make_async_remote_copy(
            src_ref=snd.at[half, owner],
            dst_ref=got.at[half, origin],
            send_sem=send_a.at[half, owner],
            recv_sem=recv_a.at[half, origin],
            device_id={"ctx": home(owner)},
            device_id_type=MESH,
        )

    def answer(half, to, owner):
        return pltpu.make_async_remote_copy(
            src_ref=ans.at[half, to],
            dst_ref=lands.at[half, owner],
            send_sem=send_b.at[half, to],
            recv_sem=recv_b.at[half, owner],
            device_id={"ctx": to},
            device_id_type=MESH,
        )

    def tile_cols(i, owner):
        return pl.ds(pl.multiple_of((i * owners + owner) * LANES, LANES), LANES)

    def send_half(half):
        def one(owner, _):
            sums = jnp.zeros((STATE, LANES), F32)
            for p in range(3):
                for j in range(part):
                    row = jnp.broadcast_to(
                        sum_s[pl.ds(p, 1), tile_cols(half * part + j, owner)], (STATE, LANES)
                    )
                    sums = jnp.where(iota((STATE, LANES), 0) == p * part + j, row, sums)
            snd[half, owner, part] = sums.astype(BF16)

            @pl.when(home(owner) != me)
            def _():
                ask(half, owner, me).start()

            return 0

        lax.fori_loop(0, owners, one, 0)

    def join(half):
        def wait(d, _):
            @pl.when(d != me)
            def _():
                ask(half, owner_me, d).wait_recv()

            return 0

        def one(d, hs):
            sums = got[half, d, part].astype(F32)
            new = []
            for j in range(part):
                ans[half, d, j] = hs[j].astype(BF16)
                total = (sums[j : j + 1] + sums[part + j : part + j + 1]) + sums[
                    2 * part + j : 2 * part + j + 1
                ]
                rate = rates[:, tile_cols(half * part + j, owner_me)]
                new.append(jnp.exp2(rate * total) * hs[j] + got[half, d, j].astype(F32))
            return tuple(new)

        def reply(d, _):
            @pl.when(d != me)
            def _():
                answer(half, d, owner_me).start()

            return 0

        @pl.when(me < owners)
        def _():
            got[half, me] = snd[half, owner_me]
            lax.fori_loop(0, size, wait, 0)
            lax.fori_loop(0, size, one, (jnp.zeros((STATE, LANES), F32),) * part, unroll=4)
            lax.fori_loop(0, size, reply, 0)
            lands[half, owner_me] = ans[half, me]

    def put_y(g):
        return pltpu.make_async_copy(xs.at[:, wide(g)], mixed_hbm.at[:, wide(g)], out_y.at[g])

    buffers = (hb0, hb1, hb2, hb3)
    zero = jnp.zeros((SUB, LANES), F32)

    def scan_group(g, _):
        cols = [pl.ds(pl.multiple_of(g * WIDE + k * LANES, LANES), LANES) for k in range(tiles)]
        lax.fori_loop(done_steps(g - 1) + 1, done_steps(g) + 1, kv_step, 0)

        if halves > 1:
            @pl.when(g == groups // 2)
            def _():
                send_half(0)

        hs = [zero] * (2 * tiles)
        for block in range(rows // BLOCK):
            first = block * BLOCK
            buffer = buffers[block % len(buffers)]
            for i in range(BLOCK):
                t = first + i
                b = [b_s[pl.ds(t * STATE + half * SUB, SUB), :] for half in range(2)]
                for k in range(tiles):
                    step = jnp.broadcast_to(step_s[pl.ds(t, 1), cols[k]], (SUB, LANES))
                    u = jnp.broadcast_to(u_s[pl.ds(t, 1), cols[k]], (SUB, LANES))
                    for half in range(2):
                        at = 2 * k + half
                        decay = jnp.exp2(step * rates[pl.ds(half * SUB, SUB), cols[k]])
                        hs[at] = decay * hs[at] + u * b[half]
                        if kept:
                            decays[g, t, at] = decay
                    buffer[k, pl.ds(i * STATE, STATE), :] = jnp.concatenate(
                        [hs[2 * k], hs[2 * k + 1]], axis=0
                    ).astype(BF16)
            for k in range(0, tiles, 2):
                pair = jnp.concatenate([buffer[k], buffer[k + 1]], axis=1)
                at = (g, pl.ds(first, BLOCK), pl.ds(k * LANES, 2 * LANES))
                y_s[at] = y_s[at] + jnp.dot(
                    c_s[pl.ds(first, BLOCK), :], pair, preferred_element_type=F32
                )
        for k in range(tiles):
            tile = g * tiles + k
            i = tile // owners
            snd[i // part, tile % owners, i % part] = jnp.concatenate(
                [hs[2 * k], hs[2 * k + 1]], axis=0
            ).astype(BF16)
        return 0

    lax.fori_loop(0, groups, scan_group, 0)
    send_half(halves - 1)
    lax.fori_loop(done_steps(groups - 1) + 1, line + 2, kv_step, 0)

    def correct_group(g, _):
        cols = [pl.ds(pl.multiple_of(g * WIDE + k * LANES, LANES), LANES) for k in range(tiles)]
        load_gate(g).wait()
        hs = []
        for k in range(tiles):
            tile = g * tiles + k
            i = tile // owners
            entering = lands[i // part, tile % owners, i % part].astype(F32)
            hs += [entering[:SUB], entering[SUB:]]
        for block in range(rows // BLOCK):
            first = block * BLOCK
            buffer = buffers[block % len(buffers)]
            for i in range(BLOCK):
                t = first + i
                for k in range(tiles):
                    for half in range(2):
                        at = 2 * k + half
                        if kept:
                            decay = decays[g, t, at]
                        else:
                            step = jnp.broadcast_to(step_s[pl.ds(t, 1), cols[k]], (SUB, LANES))
                            decay = jnp.exp2(step * rates[pl.ds(half * SUB, SUB), cols[k]])
                        hs[at] = decay * hs[at]
                    buffer[k, pl.ds(i * STATE, STATE), :] = jnp.concatenate(
                        [hs[2 * k], hs[2 * k + 1]], axis=0
                    ).astype(BF16)
            for k in range(0, tiles, 2):
                pair = jnp.concatenate([buffer[k], buffer[k + 1]], axis=1)
                both = pl.ds(pl.multiple_of(g * WIDE + k * LANES, 2 * LANES), 2 * LANES)
                at = pl.ds(first, BLOCK)
                total = y_s[g, at, pl.ds(k * LANES, 2 * LANES)] + jnp.dot(
                    c_s[at, :], pair, preferred_element_type=F32
                )
                xs[at, both] = (total * silu(raws[at, both].astype(F32))).astype(BF16)
        put_y(g).start()
        return 0

    def answers_in(half):
        def one(owner, _):
            @pl.when(home(owner) != me)
            def _():
                answer(half, me, owner).wait_recv()

            return 0

        lax.fori_loop(0, owners, one, 0)

    misc[1].wait()

    def all_arrived(i, _):
        arrived(2 * i + 1 - core)
        return 0

    lax.fori_loop(0, size // 2, all_arrived, 0)

    heads = PANEL // HEAD_DIM
    scale = LOG2E / math.sqrt(HEAD_DIM)
    wide_q = heads * rows
    full = (me * rows) // CHUNK

    def put_att(h):
        at = pl.ds(pl.multiple_of(h * PANEL, PANEL), PANEL)
        return pltpu.make_async_copy(att.at[:, at], out_hbm.at[:, at], out_a.at[h])

    def attend(h, _):
        q = jnp.concatenate(
            [
                qs[:, pl.ds(pl.multiple_of(h * PANEL + j * HEAD_DIM, HEAD_DIM), HEAD_DIM)]
                for j in range(heads)
            ],
            axis=0,
        )
        k_cols = pl.ds(pl.multiple_of(h * HEAD_DIM, HEAD_DIM), HEAD_DIM)
        v_cols = pl.ds(pl.multiple_of(KV_COLS + h * HEAD_DIM, HEAD_DIM), HEAD_DIM)

        def score(c, top, masked):
            at = pl.ds(pl.multiple_of(c * CHUNK, CHUNK), CHUNK)
            s = lax.dot_general(
                kv[at, k_cols], q, (((1,), (1,)), ((), ())), preferred_element_type=F32
            )
            if masked:
                place = c * CHUNK + iota((CHUNK, wide_q), 0)
                asker = me * rows + iota((CHUNK, wide_q), 1) % rows
                s = jnp.where(place <= asker, s, -1e30)
            sbuf[at, :] = s
            return jnp.maximum(top, jnp.max(s.reshape(CHUNK // SUB, SUB, wide_q), axis=0))

        top = jnp.full((SUB, wide_q), -1e30, F32)
        top = lax.fori_loop(0, full, lambda c, m: score(c, m, False), top)
        top = score(full, top, True)
        top = jnp.max(top, axis=0, keepdims=True) * scale

        def weigh(c, carry):
            total, summed = carry
            at = pl.ds(pl.multiple_of(c * CHUNK, CHUNK), CHUNK)
            probs = jnp.exp2(sbuf[at, :] * scale - top)
            total = total + jnp.sum(probs.reshape(CHUNK // SUB, SUB, wide_q), axis=0)
            summed = summed + lax.dot_general(
                kv[at, v_cols], probs.astype(BF16), (((0,), (0,)), ((), ())), preferred_element_type=F32
            )
            return total, summed

        total, summed = lax.fori_loop(
            0, full + 1, weigh, (jnp.zeros((SUB, wide_q), F32), jnp.zeros((HEAD_DIM, wide_q), F32))
        )
        out = (summed / jnp.sum(total, axis=0, keepdims=True)).T.astype(BF16)
        for j in range(heads):
            att[:, pl.ds(pl.multiple_of(h * PANEL + j * HEAD_DIM, HEAD_DIM), HEAD_DIM)] = out[
                j * rows : (j + 1) * rows
            ]
        put_att(h).start()
        return 0

    if halves > 1:
        join(0)
    early = EARLY
    lax.fori_loop(0, early, attend, 0)

    join(halves - 1)

    lax.fori_loop(early, KV_HEADS, attend, 0)

    half_groups = groups // halves if halves > 1 else 0
    if halves > 1:
        answers_in(0)
        lax.fori_loop(0, half_groups, correct_group, 0)
    answers_in(halves - 1)
    lax.fori_loop(half_groups, groups, correct_group, 0)

    def asked(owner, _):
        @pl.when(home(owner) != me)
        def _():
            for half in range(halves):
                ask(half, owner, me).wait_send()

        return 0

    lax.fori_loop(0, owners, asked, 0)

    @pl.when(me < owners)
    def _():
        def answered(to, _):
            @pl.when(to != me)
            def _():
                for half in range(halves):
                    answer(half, to, owner_me).wait_send()

            return 0

        lax.fori_loop(0, size, answered, 0)

    @pl.when(me + 1 < size)
    def _():
        halo_copy(me + 1).wait_send()

    def sent(i, _):
        go_across(i * LINE + within).wait_send()
        go_core(i * LINE + within).wait_send()
        go_core(i * LINE + 2 - 2 * y + core).wait_send()
        return 0

    lax.fori_loop(0, line, sent, 0)

    def sent_along(j, _):
        along(j, lambda copy: copy.wait_send())
        return 0

    lax.fori_loop(1, line, sent_along, 0)

    def written(g, _):
        put_y(g).wait()
        return 0

    lax.fori_loop(0, groups, written, 0)

    def att_written(h, _):
        put_att(h).wait()
        return 0

    lax.fori_loop(0, KV_HEADS, att_written, 0)


def per_device(
    mixer_input,
    gate_input,
    step_raw,
    input_proj,
    output_proj,
    decay_log,
    conv_weight,
    conv_bias,
    skip_gain,
    query_heads,
    key_heads,
    value_heads,
):
    rows, channels = mixer_input.shape
    size = lax.axis_size("ctx")
    groups = channels // WIDE
    line = size // LINE
    share = max(LANES, channels // size)
    owners = channels // share
    keys = rows * size
    tiles = WIDE // LANES
    own_tiles = channels // LANES // owners
    halves = 2 if own_tiles > 1 else 1
    part = own_tiles // halves
    shape = jax.ShapeDtypeStruct
    anywhere = pl.BlockSpec(memory_space=pl.ANY)
    whole = pl.BlockSpec(memory_space=pltpu.VMEM)
    dma = pltpu.SemaphoreType.DMA
    hbuf = pltpu.VMEM((WIDE // LANES, BLOCK * STATE, LANES), BF16)
    keep = keys <= 2048
    rim = -(-(TAPS - 1) * groups // HALO) * HALO

    mixer_output, attention = pl.pallas_call(
        mix_and_attend,
        in_specs=[anywhere] * 3 + [whole] * 2 + [anywhere] + [whole] * 3 + [anywhere] * 3,
        out_specs=[anywhere] * 2,
        out_shape=[shape((rows, channels), BF16), shape((rows, Q_HEADS * HEAD_DIM), BF16)],
        scratch_shapes=[
            pltpu.VMEM((rows, channels), BF16),
            pltpu.VMEM((rows, channels), BF16),
            pltpu.VMEM((STATE, channels), F32),
            pltpu.VMEM((rows, Q_HEADS * HEAD_DIM), BF16),
            pltpu.VMEM((keys, 2 * KV_COLS), BF16),
            pltpu.VMEM((rim, WIDE), BF16),
            pltpu.VMEM((rim, WIDE), BF16),
            pltpu.VMEM((rows, channels), F32),
            pltpu.VMEM((rows, channels), F32),
            pltpu.VMEM((groups, rows, WIDE), F32),
            pltpu.VMEM((3, channels), F32),
            pltpu.VMEM((rows * STATE, LANES), F32),
            pltpu.VMEM((rows, BLOCK * STATE), BF16),
            pltpu.VMEM((groups, rows, 2 * tiles, SUB, LANES) if keep else (1, 1, 1, SUB, LANES), F32),
            hbuf,
            hbuf,
            hbuf,
            hbuf,
            pltpu.VMEM((halves, owners, part + 1, STATE, LANES), BF16),
            pltpu.VMEM((halves, size, part + 1, STATE, LANES), BF16),
            pltpu.VMEM((halves, size, part, STATE, LANES), BF16),
            pltpu.VMEM((halves, owners, part, STATE, LANES), BF16),
            pltpu.VMEM((keys, PANEL // HEAD_DIM * rows), F32),
            pltpu.VMEM((rows, Q_HEADS * HEAD_DIM), BF16),
            dma((groups,)),
            dma((groups,)),
            dma((groups,)),
            dma((2,)),
            dma((2,)),
            dma,
            dma,
            dma((size,)),
            dma((line,)),
            dma((line,)),
            dma((line,)),
            dma((2 * line,)),
            dma((halves, owners)),
            dma((halves, size)),
            dma((halves, size)),
            dma((halves, owners)),
            dma((groups,)),
            dma((KV_HEADS,)),
        ],
        compiler_params=pltpu.CompilerParams(
            collective_id=0, has_side_effects=True, vmem_limit_bytes=63 * 2**20
        ),
        cost_estimate=pl.CostEstimate(
            flops=8 * rows * channels * STATE,
            bytes_accessed=8 * rows * channels,
            transcendentals=rows * channels * STATE,
        ),
        name="mix_and_attend",
    )(
        mixer_input, step_raw, gate_input, input_proj.T, output_proj.T, decay_log.T, conv_weight.T, conv_bias[None], skip_gain[None],
        query_heads, key_heads, value_heads,
    )

    return (mixer_output, attention)


def solution(mesh):
    tokens = P(("groups", "ctx"), None)
    in_specs = (tokens,) * 5 + (P(),) * 4 + (tokens,) * 3
    return jax.shard_map(
        per_device, mesh=mesh, in_specs=in_specs, out_specs=(tokens, tokens), check_vma=False
    )
```

```python
import math

import jax
import jax.numpy as jnp
from jax import lax
from jax.experimental import pallas as pl
from jax.experimental.pallas import tpu as pltpu
from jax.sharding import PartitionSpec as P

STATE = 16
TAPS = 4
Q_HEADS = 32
KV_HEADS = 4
HEAD_DIM = 128
LANES = 128
SUB = 8
HALO = 16
BLOCK = 16
WIDE = 1024
EARLY = 2
PIECES = 2
LINE = 4
KV_COLS = KV_HEADS * HEAD_DIM
PANEL = Q_HEADS // KV_HEADS * HEAD_DIM
LOG2E = math.log2(math.e)
MESH = pl.DeviceIdType.MESH
F32, BF16 = jnp.float32, jnp.bfloat16


def silu(v):
    return v / (1.0 + jnp.exp2(v * -LOG2E))


def split(v, pieces):
    out = []
    for _ in range(pieces):
        out.append(v.astype(BF16))
        v = v - out[-1].astype(F32)
    return out


def iota(shape, dim):
    return lax.broadcasted_iota(jnp.int32, shape, dim)


def spread(c_t, rows):
    depth = BLOCK * STATE
    pick = iota((STATE, depth), 1) % STATE == iota((STATE, depth), 0)
    tiled = lax.dot_general(
        c_t.astype(BF16), pick.astype(F32).astype(BF16), (((0,), (0,)), ((), ())), preferred_element_type=F32
    )
    own = iota((rows, depth), 1) // STATE == iota((rows, depth), 0) % BLOCK
    return jnp.where(own, tiled, 0.0).astype(BF16)


def mix_and_attend(
    x_hbm, raw_hbm, gate_hbm, b_ref, c_ref, decay_hbm, w_ref, bias_ref, skip_ref, q_hbm, key_hbm, value_hbm,
    mixed_hbm, out_hbm,
    xs, raws, rates, qs, kv, rim, halo, step_s, u_s, y_s, sum_s, b_s, c_s, decays, hb0, hb1, hb2, hb3,
    snd, got, ans, lands, sbuf, tops, totals, sums_s, att,
    in_x, in_raw, in_gate, in_misc, own_kv, halo_send, halo_recv,
    kv_recv, kv_up, kv_y, kv_core, send_a, recv_a, send_b, recv_b, out_y, out_a,
):
    rows, channels = x_hbm.shape
    halves, size, part, _, _ = ans.shape
    kept = decays.shape[0] > 1
    owners = lands.shape[1]
    groups = channels // WIDE
    line = size // LINE
    tiles = WIDE // LANES
    lap = owners // tiles
    me = lax.axis_index("ctx")
    z, within = me // LINE, me % LINE
    y, core = within // 2, within % 2
    across = me + 2 - 4 * y
    sibling = me + 1 - 2 * core
    barrier = pltpu.get_barrier_semaphore()

    def greet(off, _):
        pl.semaphore_signal(
            barrier, inc=1, device_id={"ctx": lax.rem(me + off, size)}, device_id_type=MESH
        )
        return 0

    lax.fori_loop(1, size, greet, 0)

    def wide(g):
        return pl.ds(pl.multiple_of(g * WIDE, WIDE), WIDE)

    def load_x(g):
        return pltpu.make_async_copy(x_hbm.at[:, wide(g)], xs.at[:, wide(g)], in_x.at[g])

    def load_raw(g):
        return pltpu.make_async_copy(raw_hbm.at[:, wide(g)], raws.at[:, wide(g)], in_raw.at[g])

    def load_gate(g):
        return pltpu.make_async_copy(gate_hbm.at[:, wide(g)], raws.at[:, wide(g)], in_gate.at[g])

    def slot(d):
        return pl.ds(pl.multiple_of(d * rows, rows), rows)

    own_copies = [
        pltpu.make_async_copy(
            source, kv.at[slot(me), pl.ds(i * KV_COLS, KV_COLS)], own_kv.at[i]
        )
        for i, source in enumerate((key_hbm, value_hbm))
    ]
    misc = [
        pltpu.make_async_copy(decay_hbm, rates, in_misc.at[0]),
        pltpu.make_async_copy(q_hbm, qs, in_misc.at[1]),
    ]

    def start_loads(g, _):
        load_raw(g).start()
        load_x(g).start()
        return 0

    lax.fori_loop(0, groups, start_loads, 0)
    for copy in own_copies + misc:
        copy.start()

    def halo_copy(to):
        return pltpu.make_async_remote_copy(
            src_ref=rim,
            dst_ref=halo,
            send_sem=halo_send,
            recv_sem=halo_recv,
            device_id={"ctx": to},
            device_id_type=MESH,
        )

    def kv_copy(origin, to, send_sem):
        return pltpu.make_async_remote_copy(
            src_ref=kv.at[slot(origin), :],
            dst_ref=kv.at[slot(origin), :],
            send_sem=send_sem,
            recv_sem=kv_recv.at[origin],
            device_id={"ctx": to},
            device_id_type=MESH,
        )

    def go_up(origin):
        return kv_copy(origin, me + LINE, kv_up.at[origin // LINE])

    def go_across(origin):
        return kv_copy(origin, across, kv_y.at[origin // LINE])

    def go_core(origin):
        return kv_copy(origin, sibling, kv_core.at[origin // 2])

    def arrived(origin):
        kv_copy(origin, sibling, kv_core.at[origin // 2]).wait_recv()

    def relay(j, _):
        origin = me - LINE * j

        @pl.when(origin >= 0)
        def _():
            arrived(origin)

            @pl.when(z < line - 1)
            def _():
                go_up(origin).start()

            go_across(origin).start()
            go_core(origin).start()

        return 0

    def cross(j, _):
        origin = across - LINE * j

        @pl.when(origin >= 0)
        def _():
            arrived(origin)
            go_core(origin).start()

        return 0

    def relayed(g):
        return jnp.minimum(((line - 1) * (g + 3)) // (groups + 1), line - 1)

    def crossed(g):
        return ((line - 1) * (g + 2)) // (groups + 1)

    pl.semaphore_wait(barrier, size - 1)
    for copy in own_copies:
        copy.wait()

    @pl.when(z < line - 1)
    def _():
        go_up(me).start()

    go_across(me).start()
    go_core(me).start()

    b_t = b_ref[...]
    for t in range(rows):
        b_s[pl.ds(t * STATE, STATE), :] = jnp.broadcast_to(b_t[:, t : t + 1], (STATE, LANES))
    c_s[...] = spread(c_ref[...], rows)

    def x_ready(g, _):
        load_x(g).wait()
        return 0

    lax.fori_loop(0, groups, x_ready, 0)
    last = xs[pl.ds(rows - HALO, HALO), :].astype(F32)
    rim_rows = [
        last[HALO - TAPS + 1 + r : HALO - TAPS + 2 + r, g * WIDE : (g + 1) * WIDE]
        for r in range(TAPS - 1)
        for g in range(groups)
    ]
    rim_rows.append(jnp.zeros((rim.shape[0] - len(rim_rows), WIDE), F32))
    rim[...] = jnp.concatenate(rim_rows, axis=0).astype(BF16)

    @pl.when(me + 1 < size)
    def _():
        halo_copy(me + 1).start()


    def shifts(height, depth, first):
        r, c = iota(((TAPS - 1) * height, depth), 0), iota(((TAPS - 1) * height, depth), 1)
        return (c == first + r % height - r // height - 1).astype(F32).astype(BF16)

    def convolve(cols, source, shift, height, first):
        moved = jnp.dot(shift, source, preferred_element_type=F32)
        conv = bias_ref[:, cols] + w_ref[pl.ds(TAPS - 1, 1), cols] * source[first : first + height].astype(F32)
        for back in range(1, TAPS):
            conv = conv + w_ref[pl.ds(TAPS - 1 - back, 1), cols] * moved[(back - 1) * height : back * height]
        return silu(conv)

    full_shift = shifts(rows, rows, 0)

    def prepare(g, _):
        load_raw(g).wait()
        cols = wide(g)
        step = jnp.log(1.0 + jnp.exp2(raws[:, cols].astype(F32) * LOG2E))
        step_s[:, cols] = step
        left = jnp.sum(step, axis=0, keepdims=True)
        for p in range(3):
            piece = left.astype(BF16).astype(F32)
            sum_s[pl.ds(p, 1), cols] = piece
            left = left - piece
        inner = convolve(cols, xs[:, cols], full_shift, rows, 0)
        u_s[:, cols] = step * inner
        y_s[g] = skip_ref[:, cols] * inner
        load_gate(g).start()
        return 0

    lax.fori_loop(0, groups, prepare, 0)
    misc[0].wait()

    def scale_rates(i, _):
        cols = pl.ds(pl.multiple_of(i * WIDE, WIDE), WIDE)
        rates[:, cols] = -LOG2E * jnp.exp2(rates[:, cols] * LOG2E)
        return 0

    lax.fori_loop(0, groups, scale_rates, 0)

    @pl.when(me > 0)
    def _():
        halo_copy(me).wait_recv()
        edge_shift = shifts(SUB, 2 * HALO, HALO)
        before = halo[...].astype(F32)
        for g in range(groups):
            cols = pl.ds(g * WIDE, WIDE)
            source = jnp.concatenate(
                [jnp.zeros((HALO - TAPS + 1, WIDE), F32)]
                + [before[r * groups + g : r * groups + g + 1] for r in range(TAPS - 1)],
                axis=0,
            ).astype(BF16)
            source = jnp.concatenate([source, xs[pl.ds(0, HALO), cols]], axis=0)
            inner = convolve(cols, source, edge_shift, SUB, HALO)
            top = pl.ds(0, SUB)
            u_s[top, cols] = step_s[top, cols] * inner
            y_s[g, top, :] = skip_ref[:, cols] * inner

    def home(owner):
        return (owner % tiles) * lap + owner // tiles

    owner_me = (me % lap) * tiles + me // lap

    def ask(half, owner, origin):
        return pltpu.make_async_remote_copy(
            src_ref=snd.at[half, owner],
            dst_ref=got.at[half, origin],
            send_sem=send_a.at[half, owner],
            recv_sem=recv_a.at[half, origin],
            device_id={"ctx": home(owner)},
            device_id_type=MESH,
        )

    def answer(half, to, owner):
        return pltpu.make_async_remote_copy(
            src_ref=ans.at[half, to],
            dst_ref=lands.at[half, owner],
            send_sem=send_b.at[half, to],
            recv_sem=recv_b.at[half, owner],
            device_id={"ctx": to},
            device_id_type=MESH,
        )

    def tile_cols(i, owner):
        return pl.ds(pl.multiple_of((i * owners + owner) * LANES, LANES), LANES)

    def send_half(half):
        def one(owner, _):
            sums = jnp.zeros((STATE, LANES), F32)
            for p in range(3):
                for j in range(part):
                    row = jnp.broadcast_to(
                        sum_s[pl.ds(p, 1), tile_cols(half * part + j, owner)], (STATE, LANES)
                    )
                    sums = jnp.where(iota((STATE, LANES), 0) == p * part + j, row, sums)
            snd[half, owner, part] = sums.astype(BF16)

            @pl.when(home(owner) != me)
            def _():
                ask(half, owner, me).start()

            return 0

        lax.fori_loop(0, owners, one, 0)

    def join(half):
        def wait(d, _):
            @pl.when(d != me)
            def _():
                ask(half, owner_me, d).wait_recv()

            return 0

        def one(d, hs):
            sums = got[half, d, part].astype(F32)
            new = []
            for j in range(part):
                ans[half, d, j] = hs[j].astype(BF16)
                total = (sums[j : j + 1] + sums[part + j : part + j + 1]) + sums[
                    2 * part + j : 2 * part + j + 1
                ]
                rate = rates[:, tile_cols(half * part + j, owner_me)]
                new.append(jnp.exp2(rate * total) * hs[j] + got[half, d, j].astype(F32))
            return tuple(new)

        def reply(d, _):
            @pl.when(d != me)
            def _():
                answer(half, d, owner_me).start()

            return 0

        @pl.when(me < owners)
        def _():
            got[half, me] = snd[half, owner_me]
            lax.fori_loop(0, size, wait, 0)
            lax.fori_loop(0, size, one, (jnp.zeros((STATE, LANES), F32),) * part, unroll=4)
            lax.fori_loop(0, size, reply, 0)
            lands[half, owner_me] = ans[half, me]

    def put_y(g):
        return pltpu.make_async_copy(xs.at[:, wide(g)], mixed_hbm.at[:, wide(g)], out_y.at[g])

    buffers = (hb0, hb1, hb2, hb3)
    zero = jnp.zeros((SUB, LANES), F32)

    def scan_group(g, _):
        cols = [pl.ds(pl.multiple_of(g * WIDE + k * LANES, LANES), LANES) for k in range(tiles)]
        lax.fori_loop(relayed(g - 1) + 1, relayed(g) + 1, relay, 0)
        lax.fori_loop(crossed(g - 1), crossed(g), cross, 0)

        if halves > 1:
            @pl.when(g == groups // 2)
            def _():
                send_half(0)

        hs = [zero] * (2 * tiles)
        for block in range(rows // BLOCK):
            first = block * BLOCK
            buffer = buffers[block % len(buffers)]
            for i in range(BLOCK):
                t = first + i
                b = [b_s[pl.ds(t * STATE + half * SUB, SUB), :] for half in range(2)]
                for k in range(tiles):
                    step = jnp.broadcast_to(step_s[pl.ds(t, 1), cols[k]], (SUB, LANES))
                    u = jnp.broadcast_to(u_s[pl.ds(t, 1), cols[k]], (SUB, LANES))
                    for half in range(2):
                        at = 2 * k + half
                        decay = jnp.exp2(step * rates[pl.ds(half * SUB, SUB), cols[k]])
                        hs[at] = decay * hs[at] + u * b[half]
                        if kept:
                            decays[g, t, at] = decay
                    buffer[k, pl.ds(i * STATE, STATE), :] = jnp.concatenate(
                        [hs[2 * k], hs[2 * k + 1]], axis=0
                    ).astype(BF16)
            for k in range(0, tiles, 2):
                pair = jnp.concatenate([buffer[k], buffer[k + 1]], axis=1)
                at = (g, pl.ds(first, BLOCK), pl.ds(k * LANES, 2 * LANES))
                y_s[at] = y_s[at] + jnp.dot(
                    c_s[pl.ds(first, BLOCK), :], pair, preferred_element_type=F32
                )
        for k in range(tiles):
            tile = g * tiles + k
            i = tile // owners
            snd[i // part, tile % owners, i % part] = jnp.concatenate(
                [hs[2 * k], hs[2 * k + 1]], axis=0
            ).astype(BF16)
        return 0

    lax.fori_loop(0, groups, scan_group, 0)
    send_half(halves - 1)

    def correct_group(g, _):
        cols = [pl.ds(pl.multiple_of(g * WIDE + k * LANES, LANES), LANES) for k in range(tiles)]
        load_gate(g).wait()
        hs = []
        for k in range(tiles):
            tile = g * tiles + k
            i = tile // owners
            entering = lands[i // part, tile % owners, i % part].astype(F32)
            hs += [entering[:SUB], entering[SUB:]]
        for block in range(rows // BLOCK):
            first = block * BLOCK
            buffer = buffers[block % len(buffers)]
            for i in range(BLOCK):
                t = first + i
                for k in range(tiles):
                    for half in range(2):
                        at = 2 * k + half
                        if kept:
                            decay = decays[g, t, at]
                        else:
                            step = jnp.broadcast_to(step_s[pl.ds(t, 1), cols[k]], (SUB, LANES))
                            decay = jnp.exp2(step * rates[pl.ds(half * SUB, SUB), cols[k]])
                        hs[at] = decay * hs[at]
                    buffer[k, pl.ds(i * STATE, STATE), :] = jnp.concatenate(
                        [hs[2 * k], hs[2 * k + 1]], axis=0
                    ).astype(BF16)
            for k in range(0, tiles, 2):
                pair = jnp.concatenate([buffer[k], buffer[k + 1]], axis=1)
                both = pl.ds(pl.multiple_of(g * WIDE + k * LANES, 2 * LANES), 2 * LANES)
                at = pl.ds(first, BLOCK)
                total = y_s[g, at, pl.ds(k * LANES, 2 * LANES)] + jnp.dot(
                    c_s[at, :], pair, preferred_element_type=F32
                )
                xs[at, both] = (total * silu(raws[at, both].astype(F32))).astype(BF16)
        put_y(g).start()
        return 0

    def answers_in(half):
        def one(owner, _):
            @pl.when(home(owner) != me)
            def _():
                answer(half, me, owner).wait_recv()

            return 0

        lax.fori_loop(0, owners, one, 0)

    misc[1].wait()

    heads = PANEL // HEAD_DIM
    scale = LOG2E / math.sqrt(HEAD_DIM)
    wide_q = heads * rows
    plane = LINE * rows

    def put_att(h):
        at = pl.ds(pl.multiple_of(h * PANEL, PANEL), PANEL)
        return pltpu.make_async_copy(att.at[:, at], out_hbm.at[:, at], out_a.at[h])

    def attend(j, own):
        c = z - j
        at = pl.ds(pl.multiple_of(c * plane, plane), plane)
        for i in range(LINE // 2):
            arrived(c * LINE + 2 * i + 1 - core)

        def one_head(h, _):
            q = jnp.concatenate(
                [
                    qs[:, pl.ds(pl.multiple_of(h * PANEL + i * HEAD_DIM, HEAD_DIM), HEAD_DIM)]
                    for i in range(heads)
                ],
                axis=0,
            )
            k_cols = pl.ds(pl.multiple_of(h * HEAD_DIM, HEAD_DIM), HEAD_DIM)
            v_cols = pl.ds(pl.multiple_of(KV_COLS + h * HEAD_DIM, HEAD_DIM), HEAD_DIM)
            s = lax.dot_general(
                kv[at, k_cols], q, (((1,), (1,)), ((), ())), preferred_element_type=F32
            )
            if own:
                place = iota((plane, wide_q), 0)
                asker = within * rows + iota((plane, wide_q), 1) % rows
                s = jnp.where(place <= asker, s, -1e30)
            sbuf[...] = s
            top = jnp.max(jnp.max(s.reshape(plane // SUB, SUB, wide_q), axis=0), axis=0, keepdims=True)
            if not own:
                old = tops[h, :1, :]
                top = jnp.maximum(top, old)
                shrink = jnp.exp2((old - top) * scale)
            tops[h, :1, :] = top
            probs = jnp.exp2(sbuf[...] * scale - top * scale)
            total = jnp.sum(probs.reshape(plane // SUB, SUB, wide_q), axis=0)
            summed = lax.dot_general(
                kv[at, v_cols], probs.astype(BF16), (((0,), (0,)), ((), ())), preferred_element_type=F32
            )
            if own:
                totals[h] = total
                sums_s[h] = summed
            else:
                totals[h] = totals[h] * shrink + total
                sums_s[h] = sums_s[h] * shrink + summed
            return 0

        lax.fori_loop(0, KV_HEADS, one_head, 0)

    def attend_plane(j, _):
        lax.fori_loop(jnp.maximum(crossed(groups - 1), j), j + 1, cross, 0)
        attend(j, False)
        return 0

    def finish_head(h, _):
        out = (sums_s[h] / jnp.sum(totals[h], axis=0, keepdims=True)).T.astype(BF16)
        for i in range(heads):
            att[:, pl.ds(pl.multiple_of(h * PANEL + i * HEAD_DIM, HEAD_DIM), HEAD_DIM)] = out[
                i * rows : (i + 1) * rows
            ]
        put_att(h).start()
        return 0

    if halves > 1:
        join(0)
    attend(0, True)
    early = jnp.minimum(z + 1, EARLY)
    lax.fori_loop(1, early, attend_plane, 0)

    join(halves - 1)

    lax.fori_loop(early, z + 1, attend_plane, 0)
    lax.fori_loop(0, KV_HEADS, finish_head, 0)

    half_groups = groups // halves if halves > 1 else 0
    if halves > 1:
        answers_in(0)
        lax.fori_loop(0, half_groups, correct_group, 0)
    answers_in(halves - 1)
    lax.fori_loop(half_groups, groups, correct_group, 0)

    def asked(owner, _):
        @pl.when(home(owner) != me)
        def _():
            for half in range(halves):
                ask(half, owner, me).wait_send()

        return 0

    lax.fori_loop(0, owners, asked, 0)

    @pl.when(me < owners)
    def _():
        def answered(to, _):
            @pl.when(to != me)
            def _():
                for half in range(halves):
                    answer(half, to, owner_me).wait_send()

            return 0

        lax.fori_loop(0, size, answered, 0)

    @pl.when(me + 1 < size)
    def _():
        halo_copy(me + 1).wait_send()

    def sent(i, _):
        @pl.when(z < line - 1)
        def _():
            go_up(i * LINE + within).wait_send()

        go_across(i * LINE + within).wait_send()
        go_core(i * LINE + within).wait_send()
        go_core(i * LINE + 2 - 2 * y + core).wait_send()
        return 0

    lax.fori_loop(0, z + 1, sent, 0)

    def written(g, _):
        put_y(g).wait()
        return 0

    lax.fori_loop(0, groups, written, 0)

    def att_written(h, _):
        put_att(h).wait()
        return 0

    lax.fori_loop(0, KV_HEADS, att_written, 0)


def hand_over(mixed_ref, attention_ref, mixed_out, attention_out):
    mixed_out[...] = mixed_ref[...]
    attention_out[...] = attention_ref[...]


def per_device(
    mixer_input,
    gate_input,
    step_raw,
    input_proj,
    output_proj,
    decay_log,
    conv_weight,
    conv_bias,
    skip_gain,
    query_heads,
    key_heads,
    value_heads,
):
    rows, channels = mixer_input.shape
    size = lax.axis_size("ctx")
    groups = channels // WIDE
    line = size // LINE
    share = max(LANES, channels // size)
    owners = channels // share
    keys = rows * size
    tiles = WIDE // LANES
    own_tiles = channels // LANES // owners
    halves = 2 if own_tiles > 1 else 1
    part = own_tiles // halves
    shape = jax.ShapeDtypeStruct
    anywhere = pl.BlockSpec(memory_space=pl.ANY)
    whole = pl.BlockSpec(memory_space=pltpu.VMEM)
    dma = pltpu.SemaphoreType.DMA
    hbuf = pltpu.VMEM((WIDE // LANES, BLOCK * STATE, LANES), BF16)
    keep = keys <= 2048
    rim = -(-(TAPS - 1) * groups // HALO) * HALO

    mixer_output, attention = pl.pallas_call(
        mix_and_attend,
        in_specs=[anywhere] * 3 + [whole] * 2 + [anywhere] + [whole] * 3 + [anywhere] * 3,
        out_specs=[anywhere] * 2,
        out_shape=[shape((rows, channels), BF16), shape((rows, Q_HEADS * HEAD_DIM), BF16)],
        scratch_shapes=[
            pltpu.VMEM((rows, channels), BF16),
            pltpu.VMEM((rows, channels), BF16),
            pltpu.VMEM((STATE, channels), F32),
            pltpu.VMEM((rows, Q_HEADS * HEAD_DIM), BF16),
            pltpu.VMEM((keys, 2 * KV_COLS), BF16),
            pltpu.VMEM((rim, WIDE), BF16),
            pltpu.VMEM((rim, WIDE), BF16),
            pltpu.VMEM((rows, channels), F32),
            pltpu.VMEM((rows, channels), F32),
            pltpu.VMEM((groups, rows, WIDE), F32),
            pltpu.VMEM((3, channels), F32),
            pltpu.VMEM((rows * STATE, LANES), F32),
            pltpu.VMEM((rows, BLOCK * STATE), BF16),
            pltpu.VMEM((groups, rows, 2 * tiles, SUB, LANES) if keep else (1, 1, 1, SUB, LANES), F32),
            hbuf,
            hbuf,
            hbuf,
            hbuf,
            pltpu.VMEM((halves, owners, part + 1, STATE, LANES), BF16),
            pltpu.VMEM((halves, size, part + 1, STATE, LANES), BF16),
            pltpu.VMEM((halves, size, part, STATE, LANES), BF16),
            pltpu.VMEM((halves, owners, part, STATE, LANES), BF16),
            pltpu.VMEM((LINE * rows, PANEL // HEAD_DIM * rows), F32),
            pltpu.VMEM((KV_HEADS, SUB, PANEL // HEAD_DIM * rows), F32),
            pltpu.VMEM((KV_HEADS, SUB, PANEL // HEAD_DIM * rows), F32),
            pltpu.VMEM((KV_HEADS, HEAD_DIM, PANEL // HEAD_DIM * rows), F32),
            pltpu.VMEM((rows, Q_HEADS * HEAD_DIM), BF16),
            dma((groups,)),
            dma((groups,)),
            dma((groups,)),
            dma((2,)),
            dma((2,)),
            dma,
            dma,
            dma((size,)),
            dma((line,)),
            dma((line,)),
            dma((2 * line,)),
            dma((halves, owners)),
            dma((halves, size)),
            dma((halves, size)),
            dma((halves, owners)),
            dma((groups,)),
            dma((KV_HEADS,)),
        ],
        compiler_params=pltpu.CompilerParams(
            collective_id=0, has_side_effects=True, vmem_limit_bytes=63 * 2**20
        ),
        cost_estimate=pl.CostEstimate(
            flops=8 * rows * channels * STATE,
            bytes_accessed=8 * rows * channels,
            transcendentals=rows * channels * STATE,
        ),
        name="mix_and_attend",
    )(
        mixer_input, step_raw, gate_input, input_proj.T, output_proj.T, decay_log.T, conv_weight.T, conv_bias[None], skip_gain[None],
        query_heads, key_heads, value_heads,
    )

    pieces = [
        pl.BlockSpec((rows, a.shape[1] // PIECES), lambda i: (0, i)) for a in (mixer_output, attention)
    ]
    return pl.pallas_call(
        hand_over,
        grid=(PIECES,),
        in_specs=pieces,
        out_specs=pieces,
        out_shape=[shape(a.shape, BF16) for a in (mixer_output, attention)],
        name="hand_over",
    )(mixer_output, attention)


def solution(mesh):
    tokens = P(("groups", "ctx"), None)
    in_specs = (tokens,) * 5 + (P(),) * 4 + (tokens,) * 3
    return jax.shard_map(
        per_device, mesh=mesh, in_specs=in_specs, out_specs=(tokens, tokens), check_vma=False
    )
```

```python
import math

import jax
import jax.numpy as jnp
from jax import lax
from jax.experimental import pallas as pl
from jax.experimental.pallas import tpu as pltpu
from jax.sharding import PartitionSpec as P

STATE = 16
TAPS = 4
Q_HEADS = 32
KV_HEADS = 4
HEAD_DIM = 128
LANES = 128
SUB = 8
HALO = 16
BLOCK = 16
WIDE = 1024
EARLY = 2
PIECES = 2
LINE = 4
KV_COLS = KV_HEADS * HEAD_DIM
PANEL = Q_HEADS // KV_HEADS * HEAD_DIM
LOG2E = math.log2(math.e)
MESH = pl.DeviceIdType.MESH
F32, BF16 = jnp.float32, jnp.bfloat16


def silu(v):
    return v / (1.0 + jnp.exp2(v * -LOG2E))


def split(v, pieces):
    out = []
    for _ in range(pieces):
        out.append(v.astype(BF16))
        v = v - out[-1].astype(F32)
    return out


def iota(shape, dim):
    return lax.broadcasted_iota(jnp.int32, shape, dim)


def spread(c_t, rows):
    depth = BLOCK * STATE
    pick = iota((STATE, depth), 1) % STATE == iota((STATE, depth), 0)
    tiled = lax.dot_general(
        c_t.astype(BF16), pick.astype(F32).astype(BF16), (((0,), (0,)), ((), ())), preferred_element_type=F32
    )
    own = iota((rows, depth), 1) // STATE == iota((rows, depth), 0) % BLOCK
    return jnp.where(own, tiled, 0.0).astype(BF16)


def mix_and_attend(
    x_hbm, raw_hbm, gate_hbm, b_ref, c_ref, decay_hbm, w_ref, bias_ref, skip_ref, q_hbm, key_hbm, value_hbm,
    mixed_hbm, out_hbm,
    xs, raws, rates, qs, kv, rim, halo, step_s, u_s, y_s, sum_s, b_s, c_s, decays, hb0, hb1, hb2, hb3,
    snd, got, ans, lands, sbuf, tops, totals, sums_s, att,
    in_x, in_raw, in_gate, in_misc, own_kv, halo_send, halo_recv,
    kv_recv, kv_up, kv_y, kv_core, send_a, recv_a, send_b, recv_b, out_y, out_a,
):
    rows, channels = x_hbm.shape
    halves, size, part, _, _ = ans.shape
    kept = decays.shape[0] > 1
    owners = lands.shape[1]
    groups = channels // WIDE
    line = size // LINE
    tiles = WIDE // LANES
    lap = owners // tiles
    me = lax.axis_index("ctx")
    z, within = me // LINE, me % LINE
    y, core = within // 2, within % 2
    across = me + 2 - 4 * y
    sibling = me + 1 - 2 * core
    barrier = pltpu.get_barrier_semaphore()

    def greet(off, _):
        pl.semaphore_signal(
            barrier, inc=1, device_id={"ctx": lax.rem(me + off, size)}, device_id_type=MESH
        )
        return 0

    lax.fori_loop(1, size, greet, 0)

    def wide(g):
        return pl.ds(pl.multiple_of(g * WIDE, WIDE), WIDE)

    def load_x(g):
        return pltpu.make_async_copy(x_hbm.at[:, wide(g)], xs.at[:, wide(g)], in_x.at[g])

    def load_raw(g):
        return pltpu.make_async_copy(raw_hbm.at[:, wide(g)], raws.at[:, wide(g)], in_raw.at[g])

    def load_gate(g):
        return pltpu.make_async_copy(gate_hbm.at[:, wide(g)], raws.at[:, wide(g)], in_gate.at[g])

    def slot(d):
        return pl.ds(pl.multiple_of(d * rows, rows), rows)

    own_copies = [
        pltpu.make_async_copy(
            source, kv.at[slot(me), pl.ds(i * KV_COLS, KV_COLS)], own_kv.at[i]
        )
        for i, source in enumerate((key_hbm, value_hbm))
    ]
    misc = [
        pltpu.make_async_copy(decay_hbm, rates, in_misc.at[0]),
        pltpu.make_async_copy(q_hbm, qs, in_misc.at[1]),
    ]

    def start_loads(g, _):
        load_raw(g).start()
        load_x(g).start()
        return 0

    lax.fori_loop(0, groups, start_loads, 0)
    for copy in own_copies + misc:
        copy.start()

    def halo_copy(to):
        return pltpu.make_async_remote_copy(
            src_ref=rim,
            dst_ref=halo,
            send_sem=halo_send,
            recv_sem=halo_recv,
            device_id={"ctx": to},
            device_id_type=MESH,
        )

    def kv_copy(origin, to, send_sem):
        return pltpu.make_async_remote_copy(
            src_ref=kv.at[slot(origin), :],
            dst_ref=kv.at[slot(origin), :],
            send_sem=send_sem,
            recv_sem=kv_recv.at[origin],
            device_id={"ctx": to},
            device_id_type=MESH,
        )

    def go_up(origin):
        return kv_copy(origin, me + LINE, kv_up.at[origin // LINE])

    def go_across(origin):
        return kv_copy(origin, across, kv_y.at[origin // LINE])

    def go_core(origin):
        return kv_copy(origin, sibling, kv_core.at[origin // 2])

    def arrived(origin):
        kv_copy(origin, sibling, kv_core.at[origin // 2]).wait_recv()

    def relay(j, _):
        origin = me - LINE * j

        @pl.when(origin >= 0)
        def _():
            arrived(origin)

            @pl.when(z < line - 1)
            def _():
                go_up(origin).start()

            go_across(origin).start()
            go_core(origin).start()

        return 0

    def cross(j, _):
        origin = across - LINE * j

        @pl.when(origin >= 0)
        def _():
            arrived(origin)
            go_core(origin).start()

        return 0

    def relayed(g):
        return ((line - 1) * (g + 4)) // (groups + 4)

    def crossed(g):
        return ((line - 1) * (g + 3)) // (groups + 4)

    pl.semaphore_wait(barrier, size - 1)
    for copy in own_copies:
        copy.wait()

    @pl.when(z < line - 1)
    def _():
        go_up(me).start()

    go_across(me).start()
    go_core(me).start()

    b_t = b_ref[...]
    for t in range(rows):
        b_s[pl.ds(t * STATE, STATE), :] = jnp.broadcast_to(b_t[:, t : t + 1], (STATE, LANES))
    c_s[...] = spread(c_ref[...], rows)

    def x_ready(g, _):
        load_x(g).wait()
        return 0

    lax.fori_loop(0, groups, x_ready, 0)
    last = xs[pl.ds(rows - HALO, HALO), :].astype(F32)
    rim_rows = [
        last[HALO - TAPS + 1 + r : HALO - TAPS + 2 + r, g * WIDE : (g + 1) * WIDE]
        for r in range(TAPS - 1)
        for g in range(groups)
    ]
    rim_rows.append(jnp.zeros((rim.shape[0] - len(rim_rows), WIDE), F32))
    rim[...] = jnp.concatenate(rim_rows, axis=0).astype(BF16)

    @pl.when(me + 1 < size)
    def _():
        halo_copy(me + 1).start()


    def shifts(height, depth, first):
        r, c = iota(((TAPS - 1) * height, depth), 0), iota(((TAPS - 1) * height, depth), 1)
        return (c == first + r % height - r // height - 1).astype(F32).astype(BF16)

    def convolve(cols, source, shift, height, first):
        moved = jnp.dot(shift, source, preferred_element_type=F32)
        conv = bias_ref[:, cols] + w_ref[pl.ds(TAPS - 1, 1), cols] * source[first : first + height].astype(F32)
        for back in range(1, TAPS):
            conv = conv + w_ref[pl.ds(TAPS - 1 - back, 1), cols] * moved[(back - 1) * height : back * height]
        return silu(conv)

    full_shift = shifts(rows, rows, 0)

    def prepare(g, _):
        load_raw(g).wait()
        cols = wide(g)
        step = jnp.log(1.0 + jnp.exp2(raws[:, cols].astype(F32) * LOG2E))
        step_s[:, cols] = step
        left = jnp.sum(step, axis=0, keepdims=True)
        for p in range(3):
            piece = left.astype(BF16).astype(F32)
            sum_s[pl.ds(p, 1), cols] = piece
            left = left - piece
        inner = convolve(cols, xs[:, cols], full_shift, rows, 0)
        u_s[:, cols] = step * inner
        y_s[g] = skip_ref[:, cols] * inner
        load_gate(g).start()
        return 0

    lax.fori_loop(0, groups, prepare, 0)
    misc[0].wait()

    def scale_rates(i, _):
        cols = pl.ds(pl.multiple_of(i * WIDE, WIDE), WIDE)
        rates[:, cols] = -LOG2E * jnp.exp2(rates[:, cols] * LOG2E)
        return 0

    lax.fori_loop(0, groups, scale_rates, 0)

    @pl.when(me > 0)
    def _():
        halo_copy(me).wait_recv()
        edge_shift = shifts(SUB, 2 * HALO, HALO)
        before = halo[...].astype(F32)
        for g in range(groups):
            cols = pl.ds(g * WIDE, WIDE)
            source = jnp.concatenate(
                [jnp.zeros((HALO - TAPS + 1, WIDE), F32)]
                + [before[r * groups + g : r * groups + g + 1] for r in range(TAPS - 1)],
                axis=0,
            ).astype(BF16)
            source = jnp.concatenate([source, xs[pl.ds(0, HALO), cols]], axis=0)
            inner = convolve(cols, source, edge_shift, SUB, HALO)
            top = pl.ds(0, SUB)
            u_s[top, cols] = step_s[top, cols] * inner
            y_s[g, top, :] = skip_ref[:, cols] * inner

    def home(owner):
        return (owner % tiles) * lap + owner // tiles

    owner_me = (me % lap) * tiles + me // lap

    def ask(half, owner, origin):
        blocks = pl.ds(0, 1 + part) if half == 0 else pl.ds(1 + half * part, part)
        return pltpu.make_async_remote_copy(
            src_ref=snd.at[owner, blocks],
            dst_ref=got.at[origin, blocks],
            send_sem=send_a.at[half, owner],
            recv_sem=recv_a.at[half, origin],
            device_id={"ctx": home(owner)},
            device_id_type=MESH,
        )

    def answer(half, to, owner):
        return pltpu.make_async_remote_copy(
            src_ref=ans.at[half, to],
            dst_ref=lands.at[half, owner],
            send_sem=send_b.at[half, to],
            recv_sem=recv_b.at[half, owner],
            device_id={"ctx": to},
            device_id_type=MESH,
        )

    own_tiles = halves * part

    def tile_cols(i, owner):
        return pl.ds(pl.multiple_of((i * owners + owner) * LANES, LANES), LANES)

    def send_half(half):
        def one(owner, _):
            if half == 0:
                sums = jnp.zeros((STATE, LANES), F32)
                for p in range(3):
                    for i in range(own_tiles):
                        row = jnp.broadcast_to(sum_s[pl.ds(p, 1), tile_cols(i, owner)], (STATE, LANES))
                        sums = jnp.where(iota((STATE, LANES), 0) == p * own_tiles + i, row, sums)
                snd[owner, 0] = sums.astype(BF16)

            @pl.when(home(owner) != me)
            def _():
                ask(half, owner, me).start()

            return 0

        lax.fori_loop(0, owners, one, 0)

    def join(half):
        def wait(d, _):
            @pl.when(d != me)
            def _():
                ask(half, owner_me, d).wait_recv()

            return 0

        def one(d, hs):
            sums = got[d, 0].astype(F32)
            new = []
            for j in range(part):
                i = half * part + j
                ans[half, d, j] = hs[j].astype(BF16)
                total = (sums[i : i + 1] + sums[own_tiles + i : own_tiles + i + 1]) + sums[
                    2 * own_tiles + i : 2 * own_tiles + i + 1
                ]
                rate = rates[:, tile_cols(i, owner_me)]
                new.append(jnp.exp2(rate * total) * hs[j] + got[d, 1 + i].astype(F32))
            return tuple(new)

        def reply(d, _):
            @pl.when(d != me)
            def _():
                answer(half, d, owner_me).start()

            return 0

        @pl.when(me < owners)
        def _():
            got[me] = snd[owner_me]
            lax.fori_loop(0, size, wait, 0)
            lax.fori_loop(0, size, one, (jnp.zeros((STATE, LANES), F32),) * part, unroll=4)
            lax.fori_loop(0, size, reply, 0)
            lands[half, owner_me] = ans[half, me]

    def put_y(g):
        return pltpu.make_async_copy(xs.at[:, wide(g)], mixed_hbm.at[:, wide(g)], out_y.at[g])

    buffers = (hb0, hb1, hb2, hb3)
    zero = jnp.zeros((SUB, LANES), F32)

    def scan_group(g, _):
        cols = [pl.ds(pl.multiple_of(g * WIDE + k * LANES, LANES), LANES) for k in range(tiles)]
        lax.fori_loop(relayed(g - 1) + 1, relayed(g) + 1, relay, 0)
        lax.fori_loop(crossed(g - 1), crossed(g), cross, 0)

        if halves > 1:
            @pl.when(g == groups // 2)
            def _():
                send_half(0)

        hs = [zero] * (2 * tiles)
        for block in range(rows // BLOCK):
            first = block * BLOCK
            buffer = buffers[block % len(buffers)]
            for i in range(BLOCK):
                t = first + i
                b = [b_s[pl.ds(t * STATE + half * SUB, SUB), :] for half in range(2)]
                for k in range(tiles):
                    step = jnp.broadcast_to(step_s[pl.ds(t, 1), cols[k]], (SUB, LANES))
                    u = jnp.broadcast_to(u_s[pl.ds(t, 1), cols[k]], (SUB, LANES))
                    for half in range(2):
                        at = 2 * k + half
                        decay = jnp.exp2(step * rates[pl.ds(half * SUB, SUB), cols[k]])
                        hs[at] = decay * hs[at] + u * b[half]
                        if kept:
                            decays[g, t, at] = decay
                    buffer[k, pl.ds(i * STATE, STATE), :] = jnp.concatenate(
                        [hs[2 * k], hs[2 * k + 1]], axis=0
                    ).astype(BF16)
            for k in range(0, tiles, 2):
                pair = jnp.concatenate([buffer[k], buffer[k + 1]], axis=1)
                at = (g, pl.ds(first, BLOCK), pl.ds(k * LANES, 2 * LANES))
                y_s[at] = y_s[at] + jnp.dot(
                    c_s[pl.ds(first, BLOCK), :], pair, preferred_element_type=F32
                )
        for k in range(tiles):
            tile = g * tiles + k
            i = tile // owners
            snd[tile % owners, 1 + i] = jnp.concatenate(
                [hs[2 * k], hs[2 * k + 1]], axis=0
            ).astype(BF16)
        return 0

    lax.fori_loop(0, groups, scan_group, 0)
    send_half(halves - 1)
    lax.fori_loop(relayed(groups - 1) + 1, line, relay, 0)

    def correct_group(g, _):
        cols = [pl.ds(pl.multiple_of(g * WIDE + k * LANES, LANES), LANES) for k in range(tiles)]
        load_gate(g).wait()
        hs = []
        for k in range(tiles):
            tile = g * tiles + k
            i = tile // owners
            entering = lands[i // part, tile % owners, i % part].astype(F32)
            hs += [entering[:SUB], entering[SUB:]]
        for block in range(rows // BLOCK):
            first = block * BLOCK
            buffer = buffers[block % len(buffers)]
            for i in range(BLOCK):
                t = first + i
                for k in range(tiles):
                    for half in range(2):
                        at = 2 * k + half
                        if kept:
                            decay = decays[g, t, at]
                        else:
                            step = jnp.broadcast_to(step_s[pl.ds(t, 1), cols[k]], (SUB, LANES))
                            decay = jnp.exp2(step * rates[pl.ds(half * SUB, SUB), cols[k]])
                        hs[at] = decay * hs[at]
                    buffer[k, pl.ds(i * STATE, STATE), :] = jnp.concatenate(
                        [hs[2 * k], hs[2 * k + 1]], axis=0
                    ).astype(BF16)
            for k in range(0, tiles, 2):
                pair = jnp.concatenate([buffer[k], buffer[k + 1]], axis=1)
                both = pl.ds(pl.multiple_of(g * WIDE + k * LANES, 2 * LANES), 2 * LANES)
                at = pl.ds(first, BLOCK)
                total = y_s[g, at, pl.ds(k * LANES, 2 * LANES)] + jnp.dot(
                    c_s[at, :], pair, preferred_element_type=F32
                )
                xs[at, both] = (total * silu(raws[at, both].astype(F32))).astype(BF16)
        put_y(g).start()
        return 0

    def answers_in(half):
        def one(owner, _):
            @pl.when(home(owner) != me)
            def _():
                answer(half, me, owner).wait_recv()

            return 0

        lax.fori_loop(0, owners, one, 0)

    misc[1].wait()

    heads = PANEL // HEAD_DIM
    scale = LOG2E / math.sqrt(HEAD_DIM)
    wide_q = heads * rows
    plane = LINE * rows

    def put_att(h):
        at = pl.ds(pl.multiple_of(h * PANEL, PANEL), PANEL)
        return pltpu.make_async_copy(att.at[:, at], out_hbm.at[:, at], out_a.at[h])

    def attend(j, own):
        c = z - j
        at = pl.ds(pl.multiple_of(c * plane, plane), plane)
        for i in range(LINE // 2):
            arrived(c * LINE + 2 * i + 1 - core)

        def one_head(h, _):
            q = jnp.concatenate(
                [
                    qs[:, pl.ds(pl.multiple_of(h * PANEL + i * HEAD_DIM, HEAD_DIM), HEAD_DIM)]
                    for i in range(heads)
                ],
                axis=0,
            )
            k_cols = pl.ds(pl.multiple_of(h * HEAD_DIM, HEAD_DIM), HEAD_DIM)
            v_cols = pl.ds(pl.multiple_of(KV_COLS + h * HEAD_DIM, HEAD_DIM), HEAD_DIM)
            s = lax.dot_general(
                kv[at, k_cols], q, (((1,), (1,)), ((), ())), preferred_element_type=F32
            )
            if own:
                place = iota((plane, wide_q), 0)
                asker = within * rows + iota((plane, wide_q), 1) % rows
                s = jnp.where(place <= asker, s, -1e30)
            sbuf[...] = s
            top = jnp.max(jnp.max(s.reshape(plane // SUB, SUB, wide_q), axis=0), axis=0, keepdims=True)
            if not own:
                old = tops[h, :1, :]
                top = jnp.maximum(top, old)
                shrink = jnp.exp2((old - top) * scale)
            tops[h, :1, :] = top
            probs = jnp.exp2(sbuf[...] * scale - top * scale)
            total = jnp.sum(probs.reshape(plane // SUB, SUB, wide_q), axis=0)
            summed = lax.dot_general(
                kv[at, v_cols], probs.astype(BF16), (((0,), (0,)), ((), ())), preferred_element_type=F32
            )
            if own:
                totals[h] = total
                sums_s[h] = summed
            else:
                totals[h] = totals[h] * shrink + total
                sums_s[h] = sums_s[h] * shrink + summed
            return 0

        lax.fori_loop(0, KV_HEADS, one_head, 0)

    def attend_plane(j, _):
        lax.fori_loop(jnp.maximum(crossed(groups - 1), j + 1), j + 2, cross, 0)
        attend(j, False)
        return 0

    def finish_head(h, _):
        out = (sums_s[h] / jnp.sum(totals[h], axis=0, keepdims=True)).T.astype(BF16)
        for i in range(heads):
            att[:, pl.ds(pl.multiple_of(h * PANEL + i * HEAD_DIM, HEAD_DIM), HEAD_DIM)] = out[
                i * rows : (i + 1) * rows
            ]
        put_att(h).start()
        return 0

    if halves > 1:
        join(0)
    attend(0, True)
    early = jnp.minimum(z + 1, EARLY)
    lax.fori_loop(1, early, attend_plane, 0)

    join(halves - 1)

    lax.fori_loop(early, z + 1, attend_plane, 0)
    lax.fori_loop(0, KV_HEADS, finish_head, 0)

    half_groups = groups // halves if halves > 1 else 0
    if halves > 1:
        answers_in(0)
        lax.fori_loop(0, half_groups, correct_group, 0)
    answers_in(halves - 1)
    lax.fori_loop(half_groups, groups, correct_group, 0)

    def asked(owner, _):
        @pl.when(home(owner) != me)
        def _():
            for half in range(halves):
                ask(half, owner, me).wait_send()

        return 0

    lax.fori_loop(0, owners, asked, 0)

    @pl.when(me < owners)
    def _():
        def answered(to, _):
            @pl.when(to != me)
            def _():
                for half in range(halves):
                    answer(half, to, owner_me).wait_send()

            return 0

        lax.fori_loop(0, size, answered, 0)

    @pl.when(me + 1 < size)
    def _():
        halo_copy(me + 1).wait_send()

    def sent(i, _):
        @pl.when(z < line - 1)
        def _():
            go_up(i * LINE + within).wait_send()

        go_across(i * LINE + within).wait_send()
        go_core(i * LINE + within).wait_send()
        go_core(i * LINE + 2 - 2 * y + core).wait_send()
        return 0

    lax.fori_loop(0, z + 1, sent, 0)

    def written(g, _):
        put_y(g).wait()
        return 0

    lax.fori_loop(0, groups, written, 0)

    def att_written(h, _):
        put_att(h).wait()
        return 0

    lax.fori_loop(0, KV_HEADS, att_written, 0)


def hand_over(mixed_hbm, attention_hbm, mixed_out, attention_out, mixed, attention, come, go):
    parts = come.shape[1]
    ways = ((mixed_hbm, mixed, mixed_out), (attention_hbm, attention, attention_out))

    def piece(way, i):
        height = ways[way][0].shape[0] // parts
        return pl.ds(i * height, height)

    order = [(way, i) for way in range(2) for i in range(parts)]
    ins = [
        pltpu.make_async_copy(ways[w][0].at[piece(w, i), :], ways[w][1].at[piece(w, i), :], come.at[w, i])
        for w, i in order
    ]
    outs = [
        pltpu.make_async_copy(ways[w][1].at[piece(w, i), :], ways[w][2].at[piece(w, i), :], go.at[w, i])
        for w, i in order
    ]
    for copy in ins:
        copy.start()
    for first, second in zip(ins, outs):
        first.wait()
        second.start()
    for copy in outs:
        copy.wait()


def per_device(
    mixer_input,
    gate_input,
    step_raw,
    input_proj,
    output_proj,
    decay_log,
    conv_weight,
    conv_bias,
    skip_gain,
    query_heads,
    key_heads,
    value_heads,
):
    rows, channels = mixer_input.shape
    size = lax.axis_size("ctx")
    groups = channels // WIDE
    line = size // LINE
    share = max(LANES, channels // size)
    owners = channels // share
    keys = rows * size
    tiles = WIDE // LANES
    own_tiles = channels // LANES // owners
    halves = 2 if own_tiles > 1 else 1
    part = own_tiles // halves
    shape = jax.ShapeDtypeStruct
    anywhere = pl.BlockSpec(memory_space=pl.ANY)
    whole = pl.BlockSpec(memory_space=pltpu.VMEM)
    dma = pltpu.SemaphoreType.DMA
    hbuf = pltpu.VMEM((WIDE // LANES, BLOCK * STATE, LANES), BF16)
    keep = keys <= 2048
    rim = -(-(TAPS - 1) * groups // HALO) * HALO

    mixer_output, attention = pl.pallas_call(
        mix_and_attend,
        in_specs=[anywhere] * 3 + [whole] * 2 + [anywhere] + [whole] * 3 + [anywhere] * 3,
        out_specs=[anywhere] * 2,
        out_shape=[shape((rows, channels), BF16), shape((rows, Q_HEADS * HEAD_DIM), BF16)],
        scratch_shapes=[
            pltpu.VMEM((rows, channels), BF16),
            pltpu.VMEM((rows, channels), BF16),
            pltpu.VMEM((STATE, channels), F32),
            pltpu.VMEM((rows, Q_HEADS * HEAD_DIM), BF16),
            pltpu.VMEM((keys, 2 * KV_COLS), BF16),
            pltpu.VMEM((rim, WIDE), BF16),
            pltpu.VMEM((rim, WIDE), BF16),
            pltpu.VMEM((rows, channels), F32),
            pltpu.VMEM((rows, channels), F32),
            pltpu.VMEM((groups, rows, WIDE), F32),
            pltpu.VMEM((3, channels), F32),
            pltpu.VMEM((rows * STATE, LANES), F32),
            pltpu.VMEM((rows, BLOCK * STATE), BF16),
            pltpu.VMEM((groups, rows, 2 * tiles, SUB, LANES) if keep else (1, 1, 1, SUB, LANES), F32),
            hbuf,
            hbuf,
            hbuf,
            hbuf,
            pltpu.VMEM((owners, own_tiles + 1, STATE, LANES), BF16),
            pltpu.VMEM((size, own_tiles + 1, STATE, LANES), BF16),
            pltpu.VMEM((halves, size, part, STATE, LANES), BF16),
            pltpu.VMEM((halves, owners, part, STATE, LANES), BF16),
            pltpu.VMEM((LINE * rows, PANEL // HEAD_DIM * rows), F32),
            pltpu.VMEM((KV_HEADS, SUB, PANEL // HEAD_DIM * rows), F32),
            pltpu.VMEM((KV_HEADS, SUB, PANEL // HEAD_DIM * rows), F32),
            pltpu.VMEM((KV_HEADS, HEAD_DIM, PANEL // HEAD_DIM * rows), F32),
            pltpu.VMEM((rows, Q_HEADS * HEAD_DIM), BF16),
            dma((groups,)),
            dma((groups,)),
            dma((groups,)),
            dma((2,)),
            dma((2,)),
            dma,
            dma,
            dma((size,)),
            dma((line,)),
            dma((line,)),
            dma((2 * line,)),
            dma((halves, owners)),
            dma((halves, size)),
            dma((halves, size)),
            dma((halves, owners)),
            dma((groups,)),
            dma((KV_HEADS,)),
        ],
        compiler_params=pltpu.CompilerParams(
            collective_id=0, has_side_effects=True, vmem_limit_bytes=63 * 2**20
        ),
        cost_estimate=pl.CostEstimate(
            flops=8 * rows * channels * STATE,
            bytes_accessed=8 * rows * channels,
            transcendentals=rows * channels * STATE,
        ),
        name="mix_and_attend",
    )(
        mixer_input, step_raw, gate_input, input_proj.T, output_proj.T, decay_log.T, conv_weight.T, conv_bias[None], skip_gain[None],
        query_heads, key_heads, value_heads,
    )

    return pl.pallas_call(
        hand_over,
        in_specs=[anywhere] * 2,
        out_specs=[anywhere] * 2,
        out_shape=[shape(a.shape, BF16) for a in (mixer_output, attention)],
        scratch_shapes=[pltpu.VMEM(a.shape, BF16) for a in (mixer_output, attention)]
        + [dma((2, PIECES))] * 2,
        name="hand_over",
    )(mixer_output, attention)


def solution(mesh):
    tokens = P(("groups", "ctx"), None)
    in_specs = (tokens,) * 5 + (P(),) * 4 + (tokens,) * 3
    return jax.shard_map(
        per_device, mesh=mesh, in_specs=in_specs, out_specs=(tokens, tokens), check_vma=False
    )
```

```python
import math

import jax
import jax.numpy as jnp
from jax import lax
from jax.experimental import pallas as pl
from jax.experimental.pallas import tpu as pltpu
from jax.sharding import PartitionSpec as P

STATE = 16
TAPS = 4
Q_HEADS = 32
KV_HEADS = 4
HEAD_DIM = 128
LANES = 128
SUB = 8
HALO = 16
BLOCK = 16
WIDE = 1024
EARLY = 2
PIECES = 2
LINE = 4
KV_COLS = KV_HEADS * HEAD_DIM
PANEL = Q_HEADS // KV_HEADS * HEAD_DIM
LOG2E = math.log2(math.e)
MESH = pl.DeviceIdType.MESH
F32, BF16 = jnp.float32, jnp.bfloat16


def silu(v):
    return v / (1.0 + jnp.exp2(v * -LOG2E))


def split(v, pieces):
    out = []
    for _ in range(pieces):
        out.append(v.astype(BF16))
        v = v - out[-1].astype(F32)
    return out


def iota(shape, dim):
    return lax.broadcasted_iota(jnp.int32, shape, dim)


def spread(c_t, rows):
    depth = BLOCK * STATE
    pick = iota((STATE, depth), 1) % STATE == iota((STATE, depth), 0)
    tiled = lax.dot_general(
        c_t.astype(BF16), pick.astype(F32).astype(BF16), (((0,), (0,)), ((), ())), preferred_element_type=F32
    )
    own = iota((rows, depth), 1) // STATE == iota((rows, depth), 0) % BLOCK
    return jnp.where(own, tiled, 0.0).astype(BF16)


def mix_and_attend(
    x_hbm, raw_hbm, gate_hbm, b_ref, c_ref, decay_hbm, w_ref, bias_ref, skip_ref, q_hbm, key_hbm, value_hbm,
    mixed_hbm, out_hbm,
    xs, raws, rates, qs, kv, rim, halo, step_s, u_s, y_s, sum_s, b_s, c_s, decays, hb0, hb1, hb2, hb3,
    snd, got, ans, lands, tops, totals, sums_s, att,
    in_x, in_raw, in_gate, in_misc, own_kv, halo_send, halo_recv,
    kv_recv, kv_up, kv_y, kv_core, send_a, recv_a, send_b, recv_b, out_y, out_a,
):
    rows, channels = x_hbm.shape
    halves, size, part, _, _ = ans.shape
    kept = decays.shape[0] > 1
    owners = lands.shape[1]
    groups = channels // WIDE
    line = size // LINE
    tiles = WIDE // LANES
    lap = owners // tiles
    me = lax.axis_index("ctx")
    z, within = me // LINE, me % LINE
    y, core = within // 2, within % 2
    across = me + 2 - 4 * y
    sibling = me + 1 - 2 * core
    barrier = pltpu.get_barrier_semaphore()

    def greet(off, _):
        pl.semaphore_signal(
            barrier, inc=1, device_id={"ctx": lax.rem(me + off, size)}, device_id_type=MESH
        )
        return 0

    lax.fori_loop(1, size, greet, 0)

    def wide(g):
        return pl.ds(pl.multiple_of(g * WIDE, WIDE), WIDE)

    def load_x(g):
        return pltpu.make_async_copy(x_hbm.at[:, wide(g)], xs.at[:, wide(g)], in_x.at[g])

    def load_raw(g):
        return pltpu.make_async_copy(raw_hbm.at[:, wide(g)], raws.at[:, wide(g)], in_raw.at[g])

    def load_gate(g):
        return pltpu.make_async_copy(gate_hbm.at[:, wide(g)], raws.at[:, wide(g)], in_gate.at[g])

    def slot(d):
        return pl.ds(pl.multiple_of(d * rows, rows), rows)

    own_copies = [
        pltpu.make_async_copy(
            source, kv.at[slot(me), pl.ds(i * KV_COLS, KV_COLS)], own_kv.at[i]
        )
        for i, source in enumerate((key_hbm, value_hbm))
    ]
    misc = [
        pltpu.make_async_copy(decay_hbm, rates, in_misc.at[0]),
        pltpu.make_async_copy(q_hbm, qs, in_misc.at[1]),
    ]

    def start_loads(g, _):
        load_raw(g).start()
        load_x(g).start()
        return 0

    lax.fori_loop(0, groups, start_loads, 0)
    for copy in own_copies + misc:
        copy.start()

    def halo_copy(to):
        return pltpu.make_async_remote_copy(
            src_ref=rim,
            dst_ref=halo,
            send_sem=halo_send,
            recv_sem=halo_recv,
            device_id={"ctx": to},
            device_id_type=MESH,
        )

    def kv_copy(origin, to, send_sem):
        return pltpu.make_async_remote_copy(
            src_ref=kv.at[slot(origin), :],
            dst_ref=kv.at[slot(origin), :],
            send_sem=send_sem,
            recv_sem=kv_recv.at[origin],
            device_id={"ctx": to},
            device_id_type=MESH,
        )

    def go_up(origin):
        return kv_copy(origin, me + LINE, kv_up.at[origin // LINE])

    def go_across(origin):
        return kv_copy(origin, across, kv_y.at[origin // LINE])

    def go_core(origin):
        return kv_copy(origin, sibling, kv_core.at[origin // 2])

    def arrived(origin):
        kv_copy(origin, sibling, kv_core.at[origin // 2]).wait_recv()

    def relay(j, _):
        origin = me - LINE * j

        @pl.when(origin >= 0)
        def _():
            arrived(origin)

            @pl.when(z < line - 1)
            def _():
                go_up(origin).start()

            go_across(origin).start()
            go_core(origin).start()

        return 0

    def cross(j, _):
        origin = across - LINE * j

        @pl.when(origin >= 0)
        def _():
            arrived(origin)
            go_core(origin).start()

        return 0

    def relayed(g):
        return ((line - 1) * (g + 4)) // (groups + 4)

    def crossed(g):
        return ((line - 1) * (g + 3)) // (groups + 4)

    pl.semaphore_wait(barrier, size - 1)
    for copy in own_copies:
        copy.wait()

    @pl.when(z < line - 1)
    def _():
        go_up(me).start()

    go_across(me).start()
    go_core(me).start()

    b_t = b_ref[...]
    for t in range(rows):
        b_s[pl.ds(t * STATE, STATE), :] = jnp.broadcast_to(b_t[:, t : t + 1], (STATE, LANES))
    c_s[...] = spread(c_ref[...], rows)

    def x_ready(g, _):
        load_x(g).wait()
        return 0

    lax.fori_loop(0, groups, x_ready, 0)
    last = xs[pl.ds(rows - HALO, HALO), :].astype(F32)
    rim_rows = [
        last[HALO - TAPS + 1 + r : HALO - TAPS + 2 + r, g * WIDE : (g + 1) * WIDE]
        for r in range(TAPS - 1)
        for g in range(groups)
    ]
    rim_rows.append(jnp.zeros((rim.shape[0] - len(rim_rows), WIDE), F32))
    rim[...] = jnp.concatenate(rim_rows, axis=0).astype(BF16)

    @pl.when(me + 1 < size)
    def _():
        halo_copy(me + 1).start()


    def shifts(height, depth, first):
        r, c = iota(((TAPS - 1) * height, depth), 0), iota(((TAPS - 1) * height, depth), 1)
        return (c == first + r % height - r // height - 1).astype(F32).astype(BF16)

    def convolve(cols, source, shift, height, first):
        moved = jnp.dot(shift, source, preferred_element_type=F32)
        conv = bias_ref[:, cols] + w_ref[pl.ds(TAPS - 1, 1), cols] * source[first : first + height].astype(F32)
        for back in range(1, TAPS):
            conv = conv + w_ref[pl.ds(TAPS - 1 - back, 1), cols] * moved[(back - 1) * height : back * height]
        return silu(conv)

    full_shift = shifts(rows, rows, 0)

    def prepare(g, _):
        load_raw(g).wait()
        cols = wide(g)
        step = jnp.log(1.0 + jnp.exp2(raws[:, cols].astype(F32) * LOG2E))
        step_s[:, cols] = step
        left = jnp.sum(step, axis=0, keepdims=True)
        for p in range(3):
            piece = left.astype(BF16).astype(F32)
            sum_s[pl.ds(p, 1), cols] = piece
            left = left - piece
        inner = convolve(cols, xs[:, cols], full_shift, rows, 0)
        u_s[:, cols] = step * inner
        y_s[g] = skip_ref[:, cols] * inner
        load_gate(g).start()
        return 0

    lax.fori_loop(0, groups, prepare, 0)
    misc[0].wait()

    def scale_rates(i, _):
        cols = pl.ds(pl.multiple_of(i * WIDE, WIDE), WIDE)
        rates[:, cols] = -LOG2E * jnp.exp2(rates[:, cols] * LOG2E)
        return 0

    lax.fori_loop(0, groups, scale_rates, 0)

    @pl.when(me > 0)
    def _():
        halo_copy(me).wait_recv()
        edge_shift = shifts(SUB, 2 * HALO, HALO)
        before = halo[...].astype(F32)
        for g in range(groups):
            cols = pl.ds(g * WIDE, WIDE)
            source = jnp.concatenate(
                [jnp.zeros((HALO - TAPS + 1, WIDE), F32)]
                + [before[r * groups + g : r * groups + g + 1] for r in range(TAPS - 1)],
                axis=0,
            ).astype(BF16)
            source = jnp.concatenate([source, xs[pl.ds(0, HALO), cols]], axis=0)
            inner = convolve(cols, source, edge_shift, SUB, HALO)
            top = pl.ds(0, SUB)
            u_s[top, cols] = step_s[top, cols] * inner
            y_s[g, top, :] = skip_ref[:, cols] * inner

    def home(owner):
        return (owner % tiles) * lap + owner // tiles

    owner_me = (me % lap) * tiles + me // lap

    def ask(half, owner, origin):
        blocks = pl.ds(0, 1 + part) if half == 0 else pl.ds(1 + half * part, part)
        return pltpu.make_async_remote_copy(
            src_ref=snd.at[owner, blocks],
            dst_ref=got.at[origin, blocks],
            send_sem=send_a.at[half, owner],
            recv_sem=recv_a.at[half, origin],
            device_id={"ctx": home(owner)},
            device_id_type=MESH,
        )

    def answer(half, to, owner):
        return pltpu.make_async_remote_copy(
            src_ref=ans.at[half, to],
            dst_ref=lands.at[half, owner],
            send_sem=send_b.at[half, to],
            recv_sem=recv_b.at[half, owner],
            device_id={"ctx": to},
            device_id_type=MESH,
        )

    own_tiles = halves * part

    def tile_cols(i, owner):
        return pl.ds(pl.multiple_of((i * owners + owner) * LANES, LANES), LANES)

    def send_half(half):
        def one(owner, _):
            if half == 0:
                sums = jnp.zeros((STATE, LANES), F32)
                for p in range(3):
                    for i in range(own_tiles):
                        row = jnp.broadcast_to(sum_s[pl.ds(p, 1), tile_cols(i, owner)], (STATE, LANES))
                        sums = jnp.where(iota((STATE, LANES), 0) == p * own_tiles + i, row, sums)
                snd[owner, 0] = sums.astype(BF16)

            @pl.when(home(owner) != me)
            def _():
                ask(half, owner, me).start()

            return 0

        lax.fori_loop(0, owners, one, 0)

    def join(half):
        def wait(d, _):
            @pl.when(d != me)
            def _():
                ask(half, owner_me, d).wait_recv()

            return 0

        def one(d, hs):
            sums = got[d, 0].astype(F32)
            new = []
            for j in range(part):
                i = half * part + j
                ans[half, d, j] = hs[j].astype(BF16)
                total = (sums[i : i + 1] + sums[own_tiles + i : own_tiles + i + 1]) + sums[
                    2 * own_tiles + i : 2 * own_tiles + i + 1
                ]
                rate = rates[:, tile_cols(i, owner_me)]
                new.append(jnp.exp2(rate * total) * hs[j] + got[d, 1 + i].astype(F32))
            return tuple(new)

        def reply(d, _):
            @pl.when(d != me)
            def _():
                answer(half, d, owner_me).start()

            return 0

        @pl.when(me < owners)
        def _():
            got[me] = snd[owner_me]
            lax.fori_loop(0, size, wait, 0)
            lax.fori_loop(0, size, one, (jnp.zeros((STATE, LANES), F32),) * part, unroll=4)
            lax.fori_loop(0, size, reply, 0)
            lands[half, owner_me] = ans[half, me]

    def put_y(g):
        return pltpu.make_async_copy(xs.at[:, wide(g)], mixed_hbm.at[:, wide(g)], out_y.at[g])

    buffers = (hb0, hb1, hb2, hb3)
    zero = jnp.zeros((SUB, LANES), F32)

    def scan_group(g, _):
        cols = [pl.ds(pl.multiple_of(g * WIDE + k * LANES, LANES), LANES) for k in range(tiles)]
        lax.fori_loop(relayed(g - 1) + 1, relayed(g) + 1, relay, 0)
        lax.fori_loop(crossed(g - 1), crossed(g), cross, 0)

        if halves > 1:
            @pl.when(g == groups // 2)
            def _():
                send_half(0)

        hs = [zero] * (2 * tiles)
        for block in range(rows // BLOCK):
            first = block * BLOCK
            buffer = buffers[block % len(buffers)]
            for i in range(BLOCK):
                t = first + i
                b = [b_s[pl.ds(t * STATE + half * SUB, SUB), :] for half in range(2)]
                for k in range(tiles):
                    step = jnp.broadcast_to(step_s[pl.ds(t, 1), cols[k]], (SUB, LANES))
                    u = jnp.broadcast_to(u_s[pl.ds(t, 1), cols[k]], (SUB, LANES))
                    for half in range(2):
                        at = 2 * k + half
                        decay = jnp.exp2(step * rates[pl.ds(half * SUB, SUB), cols[k]])
                        hs[at] = decay * hs[at] + u * b[half]
                        if kept:
                            decays[g, t, at] = decay
                    buffer[k, pl.ds(i * STATE, STATE), :] = jnp.concatenate(
                        [hs[2 * k], hs[2 * k + 1]], axis=0
                    ).astype(BF16)
            for k in range(0, tiles, 2):
                pair = jnp.concatenate([buffer[k], buffer[k + 1]], axis=1)
                at = (g, pl.ds(first, BLOCK), pl.ds(k * LANES, 2 * LANES))
                y_s[at] = y_s[at] + jnp.dot(
                    c_s[pl.ds(first, BLOCK), :], pair, preferred_element_type=F32
                )
        for k in range(tiles):
            tile = g * tiles + k
            i = tile // owners
            snd[tile % owners, 1 + i] = jnp.concatenate(
                [hs[2 * k], hs[2 * k + 1]], axis=0
            ).astype(BF16)
        return 0

    lax.fori_loop(0, groups, scan_group, 0)
    send_half(halves - 1)
    lax.fori_loop(relayed(groups - 1) + 1, line, relay, 0)

    def correct_group(g, _):
        cols = [pl.ds(pl.multiple_of(g * WIDE + k * LANES, LANES), LANES) for k in range(tiles)]
        load_gate(g).wait()
        hs = []
        for k in range(tiles):
            tile = g * tiles + k
            i = tile // owners
            entering = lands[i // part, tile % owners, i % part].astype(F32)
            hs += [entering[:SUB], entering[SUB:]]
        for block in range(rows // BLOCK):
            first = block * BLOCK
            buffer = buffers[block % len(buffers)]
            for i in range(BLOCK):
                t = first + i
                for k in range(tiles):
                    for half in range(2):
                        at = 2 * k + half
                        if kept:
                            decay = decays[g, t, at]
                        else:
                            step = jnp.broadcast_to(step_s[pl.ds(t, 1), cols[k]], (SUB, LANES))
                            decay = jnp.exp2(step * rates[pl.ds(half * SUB, SUB), cols[k]])
                        hs[at] = decay * hs[at]
                    buffer[k, pl.ds(i * STATE, STATE), :] = jnp.concatenate(
                        [hs[2 * k], hs[2 * k + 1]], axis=0
                    ).astype(BF16)
            for k in range(0, tiles, 2):
                pair = jnp.concatenate([buffer[k], buffer[k + 1]], axis=1)
                both = pl.ds(pl.multiple_of(g * WIDE + k * LANES, 2 * LANES), 2 * LANES)
                at = pl.ds(first, BLOCK)
                total = y_s[g, at, pl.ds(k * LANES, 2 * LANES)] + jnp.dot(
                    c_s[at, :], pair, preferred_element_type=F32
                )
                xs[at, both] = (total * silu(raws[at, both].astype(F32))).astype(BF16)
        put_y(g).start()
        return 0

    def answers_in(half):
        def one(owner, _):
            @pl.when(home(owner) != me)
            def _():
                answer(half, me, owner).wait_recv()

            return 0

        lax.fori_loop(0, owners, one, 0)

    misc[1].wait()

    heads = PANEL // HEAD_DIM
    scale = LOG2E / math.sqrt(HEAD_DIM)
    wide_q = heads * rows
    plane = LINE * rows

    def put_att(h):
        at = pl.ds(pl.multiple_of(h * PANEL, PANEL), PANEL)
        return pltpu.make_async_copy(att.at[:, at], out_hbm.at[:, at], out_a.at[h])

    def attend(j, own):
        c = z - j
        at = pl.ds(pl.multiple_of(c * plane, plane), plane)
        for i in range(LINE // 2):
            arrived(c * LINE + 2 * i + 1 - core)

        def one_head(h, _):
            q = jnp.concatenate(
                [
                    qs[:, pl.ds(pl.multiple_of(h * PANEL + i * HEAD_DIM, HEAD_DIM), HEAD_DIM)]
                    for i in range(heads)
                ],
                axis=0,
            )
            k_cols = pl.ds(pl.multiple_of(h * HEAD_DIM, HEAD_DIM), HEAD_DIM)
            v_cols = pl.ds(pl.multiple_of(KV_COLS + h * HEAD_DIM, HEAD_DIM), HEAD_DIM)
            s = lax.dot_general(
                kv[at, k_cols], q, (((1,), (1,)), ((), ())), preferred_element_type=F32
            )
            if own:
                place = iota((plane, wide_q), 0)
                asker = within * rows + iota((plane, wide_q), 1) % rows
                s = jnp.where(place <= asker, s, -1e30)
            top = jnp.max(jnp.max(s.reshape(plane // SUB, SUB, wide_q), axis=0), axis=0, keepdims=True)
            if not own:
                old = tops[h, :1, :]
                top = jnp.maximum(top, old)
                shrink = jnp.exp2((old - top) * scale)
            tops[h, :1, :] = top
            probs = jnp.exp2(s * scale - top * scale)
            total = jnp.sum(probs.reshape(plane // SUB, SUB, wide_q), axis=0)
            summed = lax.dot_general(
                kv[at, v_cols], probs.astype(BF16), (((0,), (0,)), ((), ())), preferred_element_type=F32
            )
            if own:
                totals[h] = total
                sums_s[h] = summed
            else:
                totals[h] = totals[h] * shrink + total
                sums_s[h] = sums_s[h] * shrink + summed
            return 0

        lax.fori_loop(0, KV_HEADS, one_head, 0, unroll=2)

    def attend_plane(j, _):
        lax.fori_loop(jnp.maximum(crossed(groups - 1), j + 1), j + 2, cross, 0)
        attend(j, False)
        return 0

    def finish_head(h, _):
        out = (sums_s[h] / jnp.sum(totals[h], axis=0, keepdims=True)).T.astype(BF16)
        for i in range(heads):
            att[:, pl.ds(pl.multiple_of(h * PANEL + i * HEAD_DIM, HEAD_DIM), HEAD_DIM)] = out[
                i * rows : (i + 1) * rows
            ]
        put_att(h).start()
        return 0

    if halves > 1:
        join(0)
    attend(0, True)
    early = jnp.minimum(z + 1, EARLY)
    lax.fori_loop(1, early, attend_plane, 0)

    join(halves - 1)

    lax.fori_loop(early, z + 1, attend_plane, 0)
    lax.fori_loop(0, KV_HEADS, finish_head, 0)

    half_groups = groups // halves if halves > 1 else 0
    if halves > 1:
        answers_in(0)
        lax.fori_loop(0, half_groups, correct_group, 0)
    answers_in(halves - 1)
    lax.fori_loop(half_groups, groups, correct_group, 0)

    def asked(owner, _):
        @pl.when(home(owner) != me)
        def _():
            for half in range(halves):
                ask(half, owner, me).wait_send()

        return 0

    lax.fori_loop(0, owners, asked, 0)

    @pl.when(me < owners)
    def _():
        def answered(to, _):
            @pl.when(to != me)
            def _():
                for half in range(halves):
                    answer(half, to, owner_me).wait_send()

            return 0

        lax.fori_loop(0, size, answered, 0)

    @pl.when(me + 1 < size)
    def _():
        halo_copy(me + 1).wait_send()

    def sent(i, _):
        @pl.when(z < line - 1)
        def _():
            go_up(i * LINE + within).wait_send()

        go_across(i * LINE + within).wait_send()
        go_core(i * LINE + within).wait_send()
        go_core(i * LINE + 2 - 2 * y + core).wait_send()
        return 0

    lax.fori_loop(0, z + 1, sent, 0)

    def written(g, _):
        put_y(g).wait()
        return 0

    lax.fori_loop(0, groups, written, 0)

    def att_written(h, _):
        put_att(h).wait()
        return 0

    lax.fori_loop(0, KV_HEADS, att_written, 0)


def hand_over(mixed_hbm, attention_hbm, mixed_out, attention_out, mixed, attention, come, go):
    parts = come.shape[1]
    ways = ((mixed_hbm, mixed, mixed_out), (attention_hbm, attention, attention_out))

    def piece(way, i):
        height = ways[way][0].shape[0] // parts
        return pl.ds(i * height, height)

    order = [(way, i) for way in range(2) for i in range(parts)]
    ins = [
        pltpu.make_async_copy(ways[w][0].at[piece(w, i), :], ways[w][1].at[piece(w, i), :], come.at[w, i])
        for w, i in order
    ]
    outs = [
        pltpu.make_async_copy(ways[w][1].at[piece(w, i), :], ways[w][2].at[piece(w, i), :], go.at[w, i])
        for w, i in order
    ]
    for copy in ins:
        copy.start()
    for first, second in zip(ins, outs):
        first.wait()
        second.start()
    for copy in outs:
        copy.wait()


def per_device(
    mixer_input,
    gate_input,
    step_raw,
    input_proj,
    output_proj,
    decay_log,
    conv_weight,
    conv_bias,
    skip_gain,
    query_heads,
    key_heads,
    value_heads,
):
    rows, channels = mixer_input.shape
    size = lax.axis_size("ctx")
    groups = channels // WIDE
    line = size // LINE
    share = max(LANES, channels // size)
    owners = channels // share
    keys = rows * size
    tiles = WIDE // LANES
    own_tiles = channels // LANES // owners
    halves = 2 if own_tiles > 1 else 1
    part = own_tiles // halves
    shape = jax.ShapeDtypeStruct
    anywhere = pl.BlockSpec(memory_space=pl.ANY)
    whole = pl.BlockSpec(memory_space=pltpu.VMEM)
    dma = pltpu.SemaphoreType.DMA
    hbuf = pltpu.VMEM((WIDE // LANES, BLOCK * STATE, LANES), BF16)
    keep = keys <= 2048
    rim = -(-(TAPS - 1) * groups // HALO) * HALO

    mixer_output, attention = pl.pallas_call(
        mix_and_attend,
        in_specs=[anywhere] * 3 + [whole] * 2 + [anywhere] + [whole] * 3 + [anywhere] * 3,
        out_specs=[anywhere] * 2,
        out_shape=[shape((rows, channels), BF16), shape((rows, Q_HEADS * HEAD_DIM), BF16)],
        scratch_shapes=[
            pltpu.VMEM((rows, channels), BF16),
            pltpu.VMEM((rows, channels), BF16),
            pltpu.VMEM((STATE, channels), F32),
            pltpu.VMEM((rows, Q_HEADS * HEAD_DIM), BF16),
            pltpu.VMEM((keys, 2 * KV_COLS), BF16),
            pltpu.VMEM((rim, WIDE), BF16),
            pltpu.VMEM((rim, WIDE), BF16),
            pltpu.VMEM((rows, channels), F32),
            pltpu.VMEM((rows, channels), F32),
            pltpu.VMEM((groups, rows, WIDE), F32),
            pltpu.VMEM((3, channels), F32),
            pltpu.VMEM((rows * STATE, LANES), F32),
            pltpu.VMEM((rows, BLOCK * STATE), BF16),
            pltpu.VMEM((groups, rows, 2 * tiles, SUB, LANES) if keep else (1, 1, 1, SUB, LANES), F32),
            hbuf,
            hbuf,
            hbuf,
            hbuf,
            pltpu.VMEM((owners, own_tiles + 1, STATE, LANES), BF16),
            pltpu.VMEM((size, own_tiles + 1, STATE, LANES), BF16),
            pltpu.VMEM((halves, size, part, STATE, LANES), BF16),
            pltpu.VMEM((halves, owners, part, STATE, LANES), BF16),
            pltpu.VMEM((KV_HEADS, SUB, PANEL // HEAD_DIM * rows), F32),
            pltpu.VMEM((KV_HEADS, SUB, PANEL // HEAD_DIM * rows), F32),
            pltpu.VMEM((KV_HEADS, HEAD_DIM, PANEL // HEAD_DIM * rows), F32),
            pltpu.VMEM((rows, Q_HEADS * HEAD_DIM), BF16),
            dma((groups,)),
            dma((groups,)),
            dma((groups,)),
            dma((2,)),
            dma((2,)),
            dma,
            dma,
            dma((size,)),
            dma((line,)),
            dma((line,)),
            dma((2 * line,)),
            dma((halves, owners)),
            dma((halves, size)),
            dma((halves, size)),
            dma((halves, owners)),
            dma((groups,)),
            dma((KV_HEADS,)),
        ],
        compiler_params=pltpu.CompilerParams(
            collective_id=0, has_side_effects=True, vmem_limit_bytes=63 * 2**20
        ),
        cost_estimate=pl.CostEstimate(
            flops=8 * rows * channels * STATE,
            bytes_accessed=8 * rows * channels,
            transcendentals=rows * channels * STATE,
        ),
        name="mix_and_attend",
    )(
        mixer_input, step_raw, gate_input, input_proj.T, output_proj.T, decay_log.T, conv_weight.T, conv_bias[None], skip_gain[None],
        query_heads, key_heads, value_heads,
    )

    return pl.pallas_call(
        hand_over,
        in_specs=[anywhere] * 2,
        out_specs=[anywhere] * 2,
        out_shape=[shape(a.shape, BF16) for a in (mixer_output, attention)],
        scratch_shapes=[pltpu.VMEM(a.shape, BF16) for a in (mixer_output, attention)]
        + [dma((2, PIECES))] * 2,
        name="hand_over",
    )(mixer_output, attention)


def solution(mesh):
    tokens = P(("groups", "ctx"), None)
    in_specs = (tokens,) * 5 + (P(),) * 4 + (tokens,) * 3
    return jax.shard_map(
        per_device, mesh=mesh, in_specs=in_specs, out_specs=(tokens, tokens), check_vma=False
    )
```
